32 devices in a mesh: grp: 2 (over y), seq: 4 (over z), tp: 4 (over x, core).
Axes of the slice: x: 2, y: 2, z: 4, core: 2. Of those that a mesh axis runs over, the one named last changes fastest.
Arguments:
- ssm_input: bfloat16 [2048, 8192], P(('grp', 'seq'), 'tp'), parts along dimension 0, may hold values from -6 to 6
- bmat: bfloat16 [2048, 1024], P(('grp', 'seq'), 'tp'), parts along dimension 0, may hold values from -6 to 6
- cmat: bfloat16 [2048, 1024], P(('grp', 'seq'), 'tp'), parts along dimension 0, may hold values from -6 to 6
- dt_raw: bfloat16 [2048, 128], P(('grp', 'seq'), 'tp'), parts along dimension 0
- a_log: float32 [128], P('tp'), may hold values from -0.5 to 0.5
- d_skip: float32 [128], P('tp'), may hold values from 0.5 to 1.5
- prompt_len: int32 [16], P('grp'), parts along dimension 0, may hold values from 1 to 1024, as said below
- owner: int32 [16], P('grp'), parts along dimension 0, may hold values from 0 to 3, as said below
- dec_x: bfloat16 [8, 4, 4, 8192], P(('grp', 'seq'), None, None, 'tp'), parts along dimension 0, may hold values from -6 to 6
- dec_b: bfloat16 [8, 4, 4, 1024], P(('grp', 'seq'), None, None, 'tp'), parts along dimension 0, may hold values from -6 to 6
- dec_c: bfloat16 [8, 4, 4, 1024], P(('grp', 'seq'), None, None, 'tp'), parts along dimension 0, may hold values from -6 to 6
- dec_dt: bfloat16 [8, 4, 4, 128], P(('grp', 'seq'), None, None, 'tp'), parts along dimension 0
Outputs:
- prefill_out: bfloat16 [2048, 8192], P(('grp', 'seq'), 'tp'), parts along dimension 0
- decode_out: bfloat16 [8, 4, 4, 8192], P(('grp', 'seq'), None, None, 'tp'), parts along dimension 0
The draws below stay inside these ranges and needn't reach their ends.
There are 2 independent parts, one for each index of `grp`. The reference program is written for one: setup_inputs(seed, part) draws one part's arguments, and reference() takes and returns one part's arrays. A program takes and returns all parts, laid end to end along the dimension named above; an argument that names none is the same for every part. Nothing has to cross between parts.
Inputs may be any that keep to these rules, and one draw needn't show every extreme that they name: `prompt_len`: no two requests have both the same owner and the same 256-position part of the prompt holding their last prompt position. Each owner decodes at most 4 requests and each part holds the last position of at most 4; some owner and some part reach that in every draw. `owner`: every index of seq owns at least one request.
All inputs are finite; a program needn't handle non-finite values.
Results may differ from the reference program's by a relative error of at most 0.0055.
Values may be sent and summed in bfloat16 or wider, within the bound.
A program may use at most 128 MiB of HBM per device.

```python
import jax
import jax.numpy as jnp
from jax import lax

H = 128
P_SIZE = 64
N = 128
G = 8
SPAN = 128
STEPS = 4
SLICE_LENGTH = 256
INPUT_LENGTH = 1024
REQUEST_COUNT = 8
N_SEQ = 4


def head_levels(key, share_slow):
    kind_key = jax.random.fold_in(key, 101)
    level_key = jax.random.fold_in(key, 102)
    slow = jax.random.uniform(kind_key, (H,)) < share_slow
    spread = jax.random.uniform(level_key, (H,))
    slow_level = jnp.exp(jnp.log(0.1) + spread * (jnp.log(0.6) - jnp.log(0.1))) / SLICE_LENGTH
    fast_level = jnp.exp(jnp.log(1.0 / 50.0) + spread * (jnp.log(1.0 / 30.0) - jnp.log(1.0 / 50.0)))
    return jnp.where(slow, slow_level, fast_level)


def draw_dt_raw(key, part):
    share_slow = 0.5
    levels = head_levels(key, share_slow)
    block_key = jax.random.fold_in(key, 103)
    rough_key = jax.random.fold_in(key, 104)
    main_random_seed = jax.random.fold_in(key, 105)
    auxiliary_random_seed = jax.random.fold_in(key, 106)
    strength_key = jax.random.fold_in(key, 107)
    block_count = INPUT_LENGTH // SLICE_LENGTH
    factor = jnp.exp(jax.random.uniform(block_key, (block_count, H), minval=jnp.log(0.5), maxval=jnp.log(2.0)))
    factor = jnp.repeat(factor, SLICE_LENGTH, axis=0)
    noise = jax.random.truncated_normal(rough_key, -2.5, 2.5, (INPUT_LENGTH, H))
    destination_device = levels[None, :] * factor * jnp.exp(0.5 * noise)
    front_stretch = jax.random.randint(main_random_seed, (), 0, SLICE_LENGTH)
    closing_stretch = jax.random.randint(auxiliary_random_seed, (), SLICE_LENGTH, INPUT_LENGTH)
    assignment_table = jnp.arange(INPUT_LENGTH)
    input_stretch = (assignment_table == front_stretch) | (assignment_table == closing_stretch)
    magnitude_level = jax.random.uniform(strength_key, (INPUT_LENGTH, H), minval=0.2, maxval=0.5)
    destination_device = jnp.where(input_stretch[:, None], magnitude_level, destination_device)
    return jnp.log(jnp.expm1(destination_device)).astype(jnp.bfloat16)


def draw_dec_dt(key, part):
    share_slow = 0.5
    levels = head_levels(key, share_slow)
    rough_key = jax.random.fold_in(key, 108)
    noise = jax.random.truncated_normal(rough_key, -2.5, 2.5, (N_SEQ, N_SEQ, STEPS, H))
    destination_device = levels * jnp.exp(0.5 * noise)
    return jnp.log(jnp.expm1(destination_device)).astype(jnp.bfloat16)


def request_table(key):
    count = N_SEQ
    pairs = count * count
    owner_key = jax.random.fold_in(key, 201)
    source_key = jax.random.fold_in(key, 202)
    score_key = jax.random.fold_in(key, 203)
    offset_key = jax.random.fold_in(key, 204)
    complete_owner = jax.random.randint(owner_key, (), 0, count)
    complete_source = jax.random.randint(source_key, (), 0, count)
    numbers = jnp.arange(pairs, dtype=jnp.int32)
    row_lookup = numbers // count
    column_lookup = numbers % count
    score_values = jax.random.randint(score_key, (pairs,), 0, 2 ** 30 // pairs) * pairs + numbers
    extra_score = jnp.where((row_lookup == complete_owner) | (column_lookup == complete_source), 2 ** 30, 0)
    sorted_ranking, picked_heads = lax.top_k(score_values + extra_score, REQUEST_COUNT)
    owners = picked_heads // count
    sources = picked_heads % count
    offsets = jax.random.randint(offset_key, (REQUEST_COUNT,), 1, SLICE_LENGTH + 1)
    lengths = sources * SLICE_LENGTH + offsets
    return (owners.astype(jnp.int32), lengths.astype(jnp.int32))


def draw_prompt_len(key, part):
    return request_table(key)[1]


def draw_owner(key, part):
    return request_table(key)[0]


def shard_levels(stream_key, shape, split, low, largest):
    factor_of = 1.0
    for position, blocks in split:
        draws = jax.random.uniform(jax.random.fold_in(jax.random.fold_in(stream_key, 6), position), (blocks,), jnp.float32, low / len(split), largest / len(split))
        factor_of = factor_of * jnp.repeat(jnp.exp(draws), shape[position] // blocks).reshape((-1,) + (1,) * (len(shape) - 1 - position))
    return factor_of


def bell_draw(rng, extent, scale, most, shards=(), held_as=jnp.bfloat16):
    result = scale * jax.random.normal(rng, extent, jnp.float32)
    if shards:
        result = result * shard_levels(rng, extent, shards, -0.22, 0.18)
    return jnp.clip(result, -most, most).astype(held_as)


def setup_inputs(seed: int = 0, part: int = 0) -> dict:
    key_list = jax.random.split(jax.random.key(seed), 13)
    part_keys = jax.random.split(jax.random.fold_in(key_list[12], part), 13)
    return {
        "ssm_input": bell_draw(part_keys[0], (INPUT_LENGTH, H * P_SIZE), 1.0, 6.0, ((0, 4), (1, 4))),
        "bmat": bell_draw(part_keys[1], (INPUT_LENGTH, G * N), 1.0, 6.0, ((0, 4), (1, 4))),
        "cmat": bell_draw(part_keys[2], (INPUT_LENGTH, G * N), 1.0, 6.0, ((0, 4), (1, 4))),
        "dt_raw": draw_dt_raw(jax.random.fold_in(jax.random.fold_in(key_list[12], part), 71), part),
        "a_log": jnp.clip(jax.random.uniform(key_list[4], (H,), jnp.float32, -0.5, 0.5) * shard_levels(key_list[4], (H,), ((0, 4),), -0.4, 0.0), -0.5, 0.5),
        "d_skip": jnp.clip(0.5 + 1.0 * jax.random.uniform(key_list[5], (H,), jnp.float32) ** shard_levels(key_list[5], (H,), ((0, 4),), -0.2, 0.2), 0.5, 1.5),
        "prompt_len": draw_prompt_len(jax.random.fold_in(jax.random.fold_in(key_list[12], part), 71), part),
        "owner": draw_owner(jax.random.fold_in(jax.random.fold_in(key_list[12], part), 71), part),
        "dec_x": bell_draw(part_keys[8], (N_SEQ, N_SEQ, STEPS, H * P_SIZE), 1.0, 6.0, ((0, 4), (3, 4))),
        "dec_b": bell_draw(part_keys[9], (N_SEQ, N_SEQ, STEPS, G * N), 1.0, 6.0, ((0, 4), (3, 4))),
        "dec_c": bell_draw(part_keys[10], (N_SEQ, N_SEQ, STEPS, G * N), 1.0, 6.0, ((0, 4), (3, 4))),
        "dec_dt": draw_dec_dt(jax.random.fold_in(jax.random.fold_in(key_list[12], part), 71), part),
    }


def reference(ssm_input, bmat, cmat, dt_raw, a_log, d_skip, prompt_len, owner, dec_x, dec_b, dec_c, dec_dt):
    highest = lax.Precision.HIGHEST
    span_count = INPUT_LENGTH // SPAN
    per_group = H // G
    step_size = jax.nn.softplus(dt_raw.astype(jnp.float32))
    log_decay = -jnp.exp(a_log)[None, :] * step_size
    cumulative = jnp.cumsum(log_decay.reshape(span_count, SPAN, H), axis=1)
    step_spans = step_size.reshape(span_count, SPAN, H)
    x_spans = ssm_input.reshape(span_count, SPAN, H, P_SIZE)
    b_spans = bmat.reshape(span_count, SPAN, G, N)
    c_spans = cmat.reshape(span_count, SPAN, G, N)
    causal = jnp.arange(SPAN)[:, None] >= jnp.arange(SPAN)[None, :]

    def span_pass(state, items):
        x_part, b_part, c_part, cum_part, step_part = items
        score_values = jnp.einsum('tgn,sgn->gts', c_part.astype(jnp.float32), b_part.astype(jnp.float32), precision=highest)
        head_scores = jnp.repeat(score_values, per_group, axis=0)
        spread = cum_part.T[:, :, None] - cum_part.T[:, None, :]
        decay = jnp.where(causal[None], jnp.exp(jnp.where(causal[None], spread, 0.0)), 0.0)
        weights = (head_scores * decay * step_part.T[:, None, :]).astype(jnp.bfloat16)
        inner = jnp.einsum('hts,shp->thp', weights.astype(jnp.float32), x_part.astype(jnp.float32), precision=highest)
        b_heads = jnp.repeat(b_part, per_group, axis=1).astype(jnp.float32)
        scaled = (b_heads * (jnp.exp(cum_part[-1][None, :] - cum_part) * step_part)[:, :, None]).astype(jnp.bfloat16)
        span_state = jnp.einsum('shp,shn->hpn', x_part.astype(jnp.float32), scaled.astype(jnp.float32), precision=highest)
        carried = jnp.einsum('tgn,gjpn->tgjp', c_part.astype(jnp.float32), state.reshape(G, per_group, P_SIZE, N), precision=highest).reshape(SPAN, H, P_SIZE)
        outer = jnp.exp(cum_part)[:, :, None] * carried
        output = (inner + outer + d_skip[None, :, None] * x_part.astype(jnp.float32)).astype(jnp.bfloat16)
        following = jnp.exp(cum_part[-1])[:, None, None] * state + span_state
        return following, (output, state)

    initial = jnp.zeros((H, P_SIZE, N), jnp.float32)
    ending, (outputs, starts) = lax.scan(span_pass, initial, (x_spans, b_spans, c_spans, cumulative, step_spans))
    prefill_out = outputs.reshape(INPUT_LENGTH, H * P_SIZE)
    rate_scale = jnp.exp(a_log)
    positions = jnp.arange(SPAN)

    def request_pass(request):
        last_token = (prompt_len[request] - 1).astype(jnp.int32)
        span_index = (last_token // SPAN).astype(jnp.int32)
        offset = (last_token % SPAN).astype(jnp.int32)
        x_part = lax.dynamic_index_in_dim(x_spans, span_index, 0, keepdims=False)
        b_part = lax.dynamic_index_in_dim(b_spans, span_index, 0, keepdims=False)
        cum_part = lax.dynamic_index_in_dim(cumulative, span_index, 0, keepdims=False)
        step_part = lax.dynamic_index_in_dim(step_spans, span_index, 0, keepdims=False)
        state = lax.dynamic_index_in_dim(starts, span_index, 0, keepdims=False)
        cum_last = lax.dynamic_index_in_dim(cum_part, offset, 0, keepdims=False)
        upto = positions[:, None] <= offset
        weight = jnp.where(upto, jnp.exp(jnp.where(upto, cum_last[None, :] - cum_part, 0.0)) * step_part, 0.0)
        b_heads = jnp.repeat(b_part, per_group, axis=1).astype(jnp.float32)
        scaled = (b_heads * weight[:, :, None]).astype(jnp.bfloat16)
        local_sum = jnp.einsum('shp,shn->hpn', x_part.astype(jnp.float32), scaled.astype(jnp.float32), precision=highest)
        handed = (jnp.exp(cum_last)[:, None, None] * state + local_sum).astype(jnp.bfloat16)
        source = (last_token // SLICE_LENGTH).astype(jnp.int32)
        holder = owner[request].astype(jnp.int32)
        slot_x = dec_x[holder, source]
        slot_b = dec_b[holder, source]
        slot_c = dec_c[holder, source]
        slot_step = dec_dt[holder, source]
        hidden = handed.astype(jnp.float32)
        rows = []
        for turn in range(STEPS):
            step_now = jax.nn.softplus(slot_step[turn].astype(jnp.float32))
            x_now = slot_x[turn].reshape(H, P_SIZE).astype(jnp.float32)
            b_now = jnp.repeat(slot_b[turn].reshape(G, N), per_group, axis=0).astype(jnp.float32)
            c_now = jnp.repeat(slot_c[turn].reshape(G, N), per_group, axis=0).astype(jnp.float32)
            hidden = jnp.exp(-rate_scale * step_now)[:, None, None] * hidden + (step_now[:, None] * x_now)[:, :, None] * b_now[:, None, :]
            reading = jnp.einsum('hpn,hn->hp', hidden, c_now, precision=highest) + d_skip[:, None] * x_now
            rows.append(reading.reshape(H * P_SIZE))
        return jnp.stack(rows).astype(jnp.bfloat16)

    decoded = lax.map(request_pass, jnp.arange(REQUEST_COUNT, dtype=jnp.int32))
    sources = ((prompt_len - 1) // SLICE_LENGTH).astype(jnp.int32)
    decode_out = jnp.zeros((N_SEQ, N_SEQ, STEPS, H * P_SIZE), jnp.bfloat16).at[owner.astype(jnp.int32), sources].set(decoded)
    return (prefill_out, decode_out)
```

```python
import functools

import jax
import jax.numpy as jnp
from jax import lax
from jax.experimental import pallas as pl
from jax.experimental.pallas import tpu as pltpu
from jax.sharding import PartitionSpec as P

H = 128
P_SIZE = 64
N = 128
G = 8
SPAN = 128
STEPS = 4
LANES = 256
MESH = pl.DeviceIdType.MESH
F32 = jnp.float32
BF16 = jnp.bfloat16
FAR = -1e30


def iota(shape, axis):
    return lax.broadcasted_iota(jnp.int32, shape, axis)


def dot(a, b):
    return jnp.dot(a, b, preferred_element_type=F32)


def dot_t(a, b):
    return lax.dot_general(a, b, (((1,), (1,)), ((), ())), preferred_element_type=F32)


def halves(value, count):
    pieces = []
    for _ in range(count):
        piece = value.astype(BF16)
        pieces.append(piece)
        value = value - piece.astype(F32)
    return pieces


def picked(selector, value, count=3):
    parts = [dot(selector, piece) for piece in halves(value, count)]
    return sum(parts[1:], parts[0])


def spread(pieces, expand):
    parts = [dot(piece, expand) for piece in pieces]
    return sum(parts[1:], parts[0])


def ones(mask):
    return jnp.where(mask, 1.0, 0.0).astype(BF16)


def softplus(value):
    return jnp.maximum(value, 0.0) + jnp.log1p(jnp.exp(-jnp.abs(value)))


def kernel(
    seq_count,
    x_ref, b_ref, c_ref, dt_ref, alog_ref, skip_ref, len_ref, own_ref,
    dx_ref, db_ref, dc_ref, ddt_ref,
    out_ref, dout_ref,
    rx, rb, rc, rdt, xd, bd, cd, dtd, res, dres, rres,
    inbuf, outbuf, first, total,
    send_in, recv_in, own_sem, send_state, recv_state, send_out, recv_out,
):
    me = lax.axis_index("seq")
    tokens, width = x_ref.shape
    heads = dt_ref.shape[1]
    groups = b_ref.shape[1] // N
    per_group = heads // groups
    spans = tokens // SPAN
    chunks = width // LANES
    heads_chunk = LANES // P_SIZE
    rows = seq_count * STEPS

    barrier = pltpu.get_barrier_semaphore()
    for d in range(1, seq_count):
        pl.semaphore_signal(
            barrier, inc=1, device_id={"seq": lax.rem(me + d, seq_count)}, device_id_type=MESH
        )
    pl.semaphore_wait(barrier, seq_count - 1)

    def exchange(source, landing, sends, recvs):
        copies = []
        for d in range(1, seq_count):
            target = lax.rem(me + d, seq_count)
            copies.append(
                pltpu.make_async_remote_copy(
                    src_ref=source.at[target],
                    dst_ref=landing.at[me],
                    send_sem=sends.at[d],
                    recv_sem=recvs.at[d],
                    device_id={"seq": target},
                    device_id_type=MESH,
                )
            )
        for copy in copies:
            copy.start()
        return copies

    arriving = []
    for k, (source, landing) in enumerate(
        ((dx_ref, rx), (db_ref, rb), (dc_ref, rc), (ddt_ref, rdt))
    ):
        arriving += exchange(source.at[0], landing, send_in.at[k], recv_in.at[k])
        mine_copy = pltpu.make_async_copy(source.at[0, me], landing.at[me], own_sem.at[k])
        mine_copy.start()
        arriving.append(mine_copy)

    step = softplus(dt_ref[...].astype(F32))
    rate = -jnp.exp(alog_ref[...])
    t_row, t_col = iota((tokens, tokens), 0), iota((tokens, tokens), 1)
    same = (t_row // SPAN) == (t_col // SPAN)
    cum = picked(ones(same & (t_col <= t_row)), rate * step)
    last = [cum[(s + 1) * SPAN - 1:(s + 1) * SPAN, :] for s in range(spans)]
    into = jnp.concatenate(
        [
            jnp.exp(last[s] - cum[s * SPAN:(s + 1) * SPAN]) * step[s * SPAN:(s + 1) * SPAN]
            for s in range(spans)
        ],
        axis=0,
    )
    into_parts = halves(into, 2)
    grown = [halves(jnp.exp(last[s]), 2) for s in range(spans)]
    outer_parts = halves(jnp.exp(cum), 2)
    cum_t = cum.T
    step_t = step.T

    def expander(chunk):
        return ones(iota((heads, LANES), 0) == iota((heads, LANES), 1) // P_SIZE + chunk * heads_chunk)

    def lanes(chunk):
        return slice(chunk * LANES, (chunk + 1) * LANES)

    b_t = [
        [b_ref[s * SPAN:(s + 1) * SPAN, g * N:(g + 1) * N].T for g in range(groups)]
        for s in range(spans)
    ]

    def onward(chunk):
        return pltpu.make_async_remote_copy(
            src_ref=outbuf.at[chunk],
            dst_ref=inbuf.at[chunk],
            send_sem=send_state.at[chunk],
            recv_sem=recv_state.at[chunk],
            device_id={"seq": lax.rem(me + 1, seq_count)},
            device_id_type=MESH,
        )

    for chunk in range(chunks):
        g = chunk * heads_chunk // per_group
        expand = expander(chunk)
        weighted = (x_ref[:, lanes(chunk)].astype(F32) * spread(into_parts, expand)).astype(BF16)
        state = None
        for s in range(spans):
            own = dot(b_t[s][g], weighted[s * SPAN:(s + 1) * SPAN])
            state = own if state is None else spread(grown[s], expand) * state + own
            if s < spans - 1:
                first[s, :, lanes(chunk)] = state
        total[:, lanes(chunk)] = state

        @pl.when(me == 0)
        def _():
            outbuf[chunk] = state.astype(BF16)
            inbuf[chunk] = jnp.zeros(inbuf.shape[1:], BF16)
            if seq_count > 1:
                onward(chunk).start()

    for copy in arriving:
        copy.wait()
    for q in range(seq_count):
        part = pl.ds(q * STEPS, STEPS)
        xd[part, :] = rx[q].astype(F32)
        bd[part, :] = rb[q].astype(F32)
        cd[part, :] = rc[q].astype(F32)
        dtd[part, :] = rdt[q].astype(F32)
    requests = len_ref.shape[1]
    final = len_ref[...] - 1
    here = (final >= me * tokens) & (final < (me + 1) * tokens)
    chosen = here & (own_ref[...] == iota((rows, requests), 0) // STEPS)
    spot = jnp.sum(jnp.where(chosen, final - me * tokens, 0), axis=1, keepdims=True)
    present = jnp.sum(jnp.where(chosen, 1, 0), axis=1, keepdims=True) > 0
    place = iota((rows, tokens), 1)
    upto = (place <= spot) & (place // SPAN == spot // SPAN)
    cum_spot = picked(ones(place == spot), cum)
    spot_span = spot // SPAN
    spot_parts = halves(jnp.exp(cum_spot), 2)
    dstep = softplus(dtd[...])
    r_row, r_col = iota((rows, rows), 0), iota((rows, rows), 1)
    slot = (r_row // STEPS) == (r_col // STEPS)
    running = picked(ones(slot & (r_col <= r_row)), rate * dstep)
    running_parts = halves(jnp.exp(running), 2)
    c_dec = cd[...].astype(BF16)
    b_dec = bd[...].astype(BF16)
    x_dec = xd[...].astype(BF16)
    head_group = iota((rows, heads), 1) // per_group
    pairs = [
        dot_t(c_dec[:, g * N:(g + 1) * N], b_dec[:, g * N:(g + 1) * N]) for g in range(groups)
    ]
    step_row = iota((rows, heads), 0) % STEPS
    fresh_parts, fresh_pick = [], []
    for k in range(STEPS):
        chosen_k = slot & (r_col % STEPS == k)
        pick = ones(chosen_k)
        score = jnp.zeros((rows, heads), F32)
        for g in range(groups):
            value = jnp.sum(jnp.where(chosen_k, pairs[g], 0.0), axis=1, keepdims=True)
            score = jnp.where(head_group == g, value, score)
        gap = jnp.where(step_row >= k, running - picked(pick, running), FAR)
        fresh_parts.append(halves(jnp.exp(gap) * picked(pick, dstep) * score, 2))
        fresh_pick.append(pick)
    skip_parts = halves(skip_ref[...], 3)

    scores, dec_scores = [], []
    for s in range(spans):
        at = slice(s * SPAN, (s + 1) * SPAN)
        scores.append([])
        dec_scores.append([])
        for g in range(groups):
            cols = slice(g * N, (g + 1) * N)
            scores[s].append(dot_t(c_ref[at, cols], b_ref[at, cols]))
            dec_scores[s].append(dot_t(c_dec[:, cols], b_ref[at, cols]))
    causal = iota((SPAN, SPAN), 0) >= iota((SPAN, SPAN), 1)
    low = ones(iota((1, 2 * P_SIZE), 1) < P_SIZE)
    high = ones(iota((1, 2 * P_SIZE), 1) >= P_SIZE)

    def weights(head, s):
        g = head // per_group
        at = slice(s * SPAN, (s + 1) * SPAN)
        row = cum_t[head:head + 1, at]
        size = step_t[head:head + 1, at]
        gap = jnp.where(causal, cum[at, head:head + 1] - row, FAR)
        main = scores[s][g] * jnp.exp(gap) * size
        gap = jnp.where(upto[:, at], cum_spot[:, head:head + 1] - row, FAR)
        extra = dec_scores[s][g] * jnp.exp(gap) * size
        return jnp.concatenate([main.astype(BF16), extra.astype(BF16)], axis=0)

    for chunk in range(chunks):
        g = chunk * heads_chunk // per_group
        cols = slice(g * N, (g + 1) * N)
        expand = expander(chunk)
        grow = [spread(grown[s], expand) for s in range(spans)]
        if seq_count > 1:

            @pl.when(me > 0)
            def _():
                onward(chunk).wait_recv()

            @pl.when((me > 0) & (me < seq_count - 1))
            def _():
                through = grow[0]
                for s in range(1, spans):
                    through = through * grow[s]
                outbuf[chunk] = (
                    through * inbuf[chunk].astype(F32) + total[:, lanes(chunk)]
                ).astype(BF16)
                onward(chunk).start()

        incoming = inbuf[chunk]
        outer = spread(outer_parts, expand)
        skip = spread(skip_parts, expand)
        from_block = None
        from_carried = None
        reach = incoming.astype(F32)
        passed = None
        for s in range(spans):
            at = slice(s * SPAN, (s + 1) * SPAN)
            inner = []
            for pair in range(heads_chunk // 2):
                head = chunk * heads_chunk + 2 * pair
                start = chunk * LANES + pair * 2 * P_SIZE
                x_pair = x_ref[at, start:start + 2 * P_SIZE]
                both = jnp.concatenate([x_pair * low, x_pair * high], axis=0)
                left = jnp.concatenate([weights(head, s), weights(head + 1, s)], axis=1)
                inner.append(dot(left, both))
            inner = jnp.concatenate(inner, axis=1)
            if s == 0:
                held = incoming
            else:
                passed = grow[s - 1] if passed is None else passed * grow[s - 1]
                held = (passed * reach + first[s - 1, :, lanes(chunk)]).astype(BF16)
            carried = dot(jnp.concatenate([c_ref[at, cols], c_dec[:, cols]], axis=0), held)
            x_part = x_ref[at, lanes(chunk)].astype(F32)
            out_ref[at, lanes(chunk)] = (
                inner[:SPAN] + outer[at] * carried[:SPAN] + skip * x_part
            ).astype(BF16)
            from_block = inner[SPAN:] if s == 0 else from_block + inner[SPAN:]
            from_carried = (
                carried[SPAN:]
                if s == 0
                else jnp.where(spot_span == s, carried[SPAN:], from_carried)
            )
        state_part = spread(spot_parts, expand) * from_carried + from_block
        xd_part = x_dec[:, lanes(chunk)]
        value = spread(running_parts, expand) * state_part + skip * xd_part.astype(F32)
        for k in range(STEPS):
            value = value + spread(fresh_parts[k], expand) * dot(fresh_pick[k], xd_part)
        res[:, lanes(chunk)] = jnp.where(present, value, 0.0)

    for q in range(seq_count):
        dres[q] = res[pl.ds(q * STEPS, STEPS), :].astype(BF16)
    leaving = exchange(dres, rres, send_out, recv_out)
    mine_copy = pltpu.make_async_copy(dres.at[me], rres.at[me], own_sem.at[0])
    mine_copy.start()
    for copy in leaving + [mine_copy]:
        copy.wait()
    dout_ref[0] = rres[...]
    if seq_count > 1:

        @pl.when(me < seq_count - 1)
        def _():
            for chunk in range(chunks):
                onward(chunk).wait_send()


def shards(
    ssm_input, bmat, cmat, dt_raw, a_log, d_skip, prompt_len, owner, dec_x, dec_b, dec_c, dec_dt
):
    seq_count = lax.axis_size("seq")
    tokens, width = ssm_input.shape
    heads = dt_raw.shape[1]
    gn = bmat.shape[1]
    spans = tokens // SPAN
    chunks = width // LANES
    rows = seq_count * STEPS
    vmem = pl.BlockSpec(memory_space=pltpu.VMEM)
    dma = pltpu.SemaphoreType.DMA
    slots = (seq_count, STEPS)
    return pl.pallas_call(
        functools.partial(kernel, seq_count),
        out_shape=(
            jax.ShapeDtypeStruct((tokens, width), BF16),
            jax.ShapeDtypeStruct((1,) + slots + (width,), BF16),
        ),
        in_specs=[vmem] * 12,
        out_specs=(vmem, vmem),
        scratch_shapes=[
            pltpu.VMEM(slots + (width,), BF16),
            pltpu.VMEM(slots + (gn,), BF16),
            pltpu.VMEM(slots + (gn,), BF16),
            pltpu.VMEM(slots + (heads,), BF16),
            pltpu.VMEM((rows, width), F32),
            pltpu.VMEM((rows, gn), F32),
            pltpu.VMEM((rows, gn), F32),
            pltpu.VMEM((rows, heads), F32),
            pltpu.VMEM((rows, width), F32),
            pltpu.VMEM(slots + (width,), BF16),
            pltpu.VMEM(slots + (width,), BF16),
            pltpu.VMEM((chunks, N, LANES), BF16),
            pltpu.VMEM((chunks, N, LANES), BF16),
            pltpu.VMEM((max(spans - 1, 1), N, width), F32),
            pltpu.VMEM((N, width), F32),
            dma((4, seq_count)),
            dma((4, seq_count)),
            dma((4,)),
            dma((chunks,)),
            dma((chunks,)),
            dma((seq_count,)),
            dma((seq_count,)),
        ],
        compiler_params=pltpu.CompilerParams(
            collective_id=0, has_side_effects=True, vmem_limit_bytes=40 * 1024 * 1024
        ),
    )(
        ssm_input, bmat, cmat, dt_raw, a_log[None, :], d_skip[None, :],
        prompt_len[None, :], owner[None, :], dec_x, dec_b, dec_c, dec_dt,
    )


def solution(mesh):
    placed = (
        P(("grp", "seq"), "tp"),
        P(("grp", "seq"), "tp"),
        P(("grp", "seq"), "tp"),
        P(("grp", "seq"), "tp"),
        P("tp"),
        P("tp"),
        P("grp"),
        P("grp"),
        P(("grp", "seq"), None, None, "tp"),
        P(("grp", "seq"), None, None, "tp"),
        P(("grp", "seq"), None, None, "tp"),
        P(("grp", "seq"), None, None, "tp"),
    )
    return jax.shard_map(
        shards,
        mesh=mesh,
        in_specs=placed,
        out_specs=(P(("grp", "seq"), "tp"), P(("grp", "seq"), None, None, "tp")),
        check_vma=False,
    )
```

```python
import functools

import jax
import jax.numpy as jnp
from jax import lax
from jax.experimental import pallas as pl
from jax.experimental.pallas import tpu as pltpu
from jax.sharding import PartitionSpec as P

H = 128
P_SIZE = 64
N = 128
G = 8
SPAN = 128
STEPS = 4
LANES = 256
HOP = 128
MESH = pl.DeviceIdType.MESH
F32 = jnp.float32
BF16 = jnp.bfloat16
FAR = -1e30


def iota(shape, axis):
    return lax.broadcasted_iota(jnp.int32, shape, axis)


def dot(a, b):
    return jnp.dot(a, b, preferred_element_type=F32)


def dot_t(a, b):
    return lax.dot_general(a, b, (((1,), (1,)), ((), ())), preferred_element_type=F32)


def halves(value, count):
    pieces = []
    for _ in range(count):
        piece = value.astype(BF16)
        pieces.append(piece)
        value = value - piece.astype(F32)
    return pieces


def picked(selector, value, count=3):
    parts = [dot(selector, piece) for piece in halves(value, count)]
    return sum(parts[1:], parts[0])


def spread(pieces, expand):
    parts = [dot(piece, expand) for piece in pieces]
    return sum(parts[1:], parts[0])


def ones(mask):
    return jnp.where(mask, 1.0, 0.0).astype(BF16)


def softplus(value):
    return jnp.maximum(value, 0.0) + jnp.log1p(jnp.exp(-jnp.abs(value)))


def kernel(
    seq_count,
    x_hbm, b_hbm, c_hbm, dt_ref, alog_ref, skip_ref, len_ref, own_ref,
    dx_ref, db_ref, dc_ref, ddt_ref,
    out_ref, dout_ref,
    x_ref, b_ref, c_ref, rx, rb, rc, rdt, xd, bd, cd, dtd, res, dres, rres,
    inbuf, outbuf, first, total,
    load_sem, send_in, recv_in, own_sem, send_state, recv_state, send_out, recv_out,
):
    me = lax.axis_index("seq")
    tokens, width = x_ref.shape
    heads = dt_ref.shape[0]
    groups = b_ref.shape[1] // N
    per_group = heads // groups
    spans = tokens // SPAN
    chunks = width // LANES
    heads_chunk = LANES // P_SIZE
    rows = seq_count * STEPS

    barrier = pltpu.get_barrier_semaphore()
    for d in range(1, seq_count):
        pl.semaphore_signal(
            barrier, inc=1, device_id={"seq": lax.rem(me + d, seq_count)}, device_id_type=MESH
        )
    loads = [
        pltpu.make_async_copy(source, landing, load_sem.at[k])
        for k, (source, landing) in enumerate(((x_hbm, x_ref), (b_hbm, b_ref), (c_hbm, c_ref)))
    ]
    for copy in loads:
        copy.start()

    step_t = softplus(dt_ref[...].astype(F32))
    step = step_t.T
    rate = -jnp.exp(alog_ref[...])
    t_row, t_col = iota((tokens, tokens), 0), iota((tokens, tokens), 1)
    same = (t_row // SPAN) == (t_col // SPAN)
    cum = picked(ones(same & (t_col <= t_row)), rate * step)
    last = [cum[(s + 1) * SPAN - 1:(s + 1) * SPAN, :] for s in range(spans)]
    into = jnp.concatenate(
        [
            jnp.exp(last[s] - cum[s * SPAN:(s + 1) * SPAN]) * step[s * SPAN:(s + 1) * SPAN]
            for s in range(spans)
        ],
        axis=0,
    )
    into_parts = halves(into, 2)
    grown = [halves(jnp.exp(last[s]), 2) for s in range(spans)]
    outer_parts = halves(jnp.exp(cum), 2)
    cum_t = cum.T

    def exchange(source, landing, sends, recvs):
        copies = []
        for d in range(1, seq_count):
            target = lax.rem(me + d, seq_count)
            copies.append(
                pltpu.make_async_remote_copy(
                    src_ref=source.at[target],
                    dst_ref=landing.at[me],
                    send_sem=sends.at[d],
                    recv_sem=recvs.at[d],
                    device_id={"seq": target},
                    device_id_type=MESH,
                )
            )
        for copy in copies:
            copy.start()
        return copies

    def expander(chunk):
        return ones(iota((heads, LANES), 0) == iota((heads, LANES), 1) // P_SIZE + chunk * heads_chunk)

    def lanes(chunk):
        return slice(chunk * LANES, (chunk + 1) * LANES)

    for copy in loads:
        copy.wait()
    pl.semaphore_wait(barrier, seq_count - 1)
    b_t = [
        [b_ref[s * SPAN:(s + 1) * SPAN, g * N:(g + 1) * N].T for g in range(groups)]
        for s in range(spans)
    ]
    hops = width // HOP

    def hop_lanes(hop):
        return slice(hop * HOP, (hop + 1) * HOP)

    def onward(hop):
        return pltpu.make_async_remote_copy(
            src_ref=outbuf.at[hop],
            dst_ref=inbuf.at[hop],
            send_sem=send_state.at[hop],
            recv_sem=recv_state.at[hop],
            device_id={"seq": lax.rem(me + 1, seq_count)},
            device_id_type=MESH,
        )

    for chunk in range(chunks):
        g = chunk * heads_chunk // per_group
        expand = expander(chunk)
        weighted = (x_ref[:, lanes(chunk)].astype(F32) * spread(into_parts, expand)).astype(BF16)
        state = None
        for s in range(spans):
            own = dot(b_t[s][g], weighted[s * SPAN:(s + 1) * SPAN])
            state = own if state is None else spread(grown[s], expand) * state + own
            if s < spans - 1:
                first[s, :, lanes(chunk)] = state
        total[:, lanes(chunk)] = state

        @pl.when(me == 0)
        def _():
            for part in range(LANES // HOP):
                hop = chunk * (LANES // HOP) + part
                outbuf[hop] = state[:, hop_lanes(part)].astype(BF16)
                inbuf[hop] = jnp.zeros(inbuf.shape[1:], BF16)
                if seq_count > 1:
                    onward(hop).start()

    def relay(hop):
        if seq_count == 1 or hop >= hops:
            return
        chunk, part = hop * HOP // LANES, hop % (LANES // HOP)

        @pl.when((me > 0) & (me < seq_count - 1))
        def _():
            onward(hop).wait_recv()
            expand = expander(chunk)[:, hop_lanes(part)]
            through = spread(grown[0], expand)
            for s in range(1, spans):
                through = through * spread(grown[s], expand)
            outbuf[hop] = (
                through * inbuf[hop].astype(F32) + total[:, hop_lanes(hop)]
            ).astype(BF16)
            onward(hop).start()

    arriving = []
    for k, (source, landing) in enumerate(
        ((dx_ref, rx), (db_ref, rb), (dc_ref, rc), (ddt_ref, rdt))
    ):
        arriving += exchange(source.at[0], landing, send_in.at[k], recv_in.at[k])
        mine_copy = pltpu.make_async_copy(source.at[0, me], landing.at[me], own_sem.at[k])
        mine_copy.start()
        arriving.append(mine_copy)

    for hop in range(LANES // HOP):
        relay(hop)

    for copy in arriving:
        copy.wait()
    for q in range(seq_count):
        part = pl.ds(q * STEPS, STEPS)
        xd[part, :] = rx[q].astype(F32)
        bd[part, :] = rb[q].astype(F32)
        cd[part, :] = rc[q].astype(F32)
        dtd[part, :] = rdt[q].astype(F32)
    requests = len_ref.shape[1]
    final = len_ref[...] - 1
    here = (final >= me * tokens) & (final < (me + 1) * tokens)
    chosen = here & (own_ref[...] == iota((rows, requests), 0) // STEPS)
    spot = jnp.sum(jnp.where(chosen, final - me * tokens, 0), axis=1, keepdims=True)
    present = jnp.sum(jnp.where(chosen, 1, 0), axis=1, keepdims=True) > 0
    place = iota((rows, tokens), 1)
    upto = (place <= spot) & (place // SPAN == spot // SPAN)
    cum_spot = picked(ones(place == spot), cum)
    spot_span = spot // SPAN
    spot_parts = halves(jnp.exp(cum_spot), 2)
    dstep = softplus(dtd[...])
    r_row, r_col = iota((rows, rows), 0), iota((rows, rows), 1)
    slot = (r_row // STEPS) == (r_col // STEPS)
    running = picked(ones(slot & (r_col <= r_row)), rate * dstep)
    running_parts = halves(jnp.exp(running), 2)
    c_dec = cd[...].astype(BF16)
    b_dec = bd[...].astype(BF16)
    x_dec = xd[...].astype(BF16)
    head_group = iota((rows, heads), 1) // per_group
    pairs = [
        dot_t(c_dec[:, g * N:(g + 1) * N], b_dec[:, g * N:(g + 1) * N]) for g in range(groups)
    ]
    step_row = iota((rows, heads), 0) % STEPS
    fresh_parts, fresh_pick = [], []
    for k in range(STEPS):
        chosen_k = slot & (r_col % STEPS == k)
        pick = ones(chosen_k)
        score = jnp.zeros((rows, heads), F32)
        for g in range(groups):
            value = jnp.sum(jnp.where(chosen_k, pairs[g], 0.0), axis=1, keepdims=True)
            score = jnp.where(head_group == g, value, score)
        gap = jnp.where(step_row >= k, running - picked(pick, running), FAR)
        fresh_parts.append(halves(jnp.exp(gap) * picked(pick, dstep) * score, 2))
        fresh_pick.append(pick)
    skip_parts = halves(skip_ref[...], 3)

    scores, dec_scores = [], []
    for s in range(spans):
        at = slice(s * SPAN, (s + 1) * SPAN)
        scores.append([])
        dec_scores.append([])
        for g in range(groups):
            cols = slice(g * N, (g + 1) * N)
            scores[s].append(dot_t(c_ref[at, cols], b_ref[at, cols]))
            dec_scores[s].append(dot_t(c_dec[:, cols], b_ref[at, cols]))
    causal = iota((SPAN, SPAN), 0) >= iota((SPAN, SPAN), 1)
    low = ones(iota((1, 2 * P_SIZE), 1) < P_SIZE)
    high = ones(iota((1, 2 * P_SIZE), 1) >= P_SIZE)

    def weights(head, s):
        g = head // per_group
        at = slice(s * SPAN, (s + 1) * SPAN)
        row = cum_t[head:head + 1, at]
        size = step_t[head:head + 1, at]
        gap = jnp.where(causal, cum[at, head:head + 1] - row, FAR)
        main = scores[s][g] * jnp.exp(gap) * size
        gap = jnp.where(upto[:, at], cum_spot[:, head:head + 1] - row, FAR)
        extra = dec_scores[s][g] * jnp.exp(gap) * size
        return jnp.concatenate([main.astype(BF16), extra.astype(BF16)], axis=0)

    ends = [chunks // 2, chunks - 1, chunks]
    leaving = []
    for chunk in range(chunks):
        g = chunk * heads_chunk // per_group
        cols = slice(g * N, (g + 1) * N)
        expand = expander(chunk)
        grow = [spread(grown[s], expand) for s in range(spans)]
        inners = []
        for s in range(spans):
            at = slice(s * SPAN, (s + 1) * SPAN)
            inner = []
            for pair in range(heads_chunk // 2):
                head = chunk * heads_chunk + 2 * pair
                start = chunk * LANES + pair * 2 * P_SIZE
                x_pair = x_ref[at, start:start + 2 * P_SIZE]
                both = jnp.concatenate([x_pair * low, x_pair * high], axis=0)
                left = jnp.concatenate([weights(head, s), weights(head + 1, s)], axis=1)
                inner.append(dot(left, both))
            inners.append(jnp.concatenate(inner, axis=1))
        hop = chunk * (LANES // HOP)
        for part in range(LANES // HOP // 2):
            relay(hop + LANES // HOP + part)
        if seq_count > 1:

            @pl.when(me == seq_count - 1)
            def _():
                for part in range(LANES // HOP):
                    onward(hop + part).wait_recv()

        incoming = jnp.concatenate([inbuf[hop + part] for part in range(LANES // HOP)], axis=1)
        outer = spread(outer_parts, expand)
        skip = spread(skip_parts, expand)
        from_block = None
        from_carried = None
        reach = incoming.astype(F32)
        passed = None
        for s in range(spans):
            at = slice(s * SPAN, (s + 1) * SPAN)
            inner = inners[s]
            if s == 0:
                held = incoming
            else:
                passed = grow[s - 1] if passed is None else passed * grow[s - 1]
                held = (passed * reach + first[s - 1, :, lanes(chunk)]).astype(BF16)
            carried = dot(jnp.concatenate([c_ref[at, cols], c_dec[:, cols]], axis=0), held)
            x_part = x_ref[at, lanes(chunk)].astype(F32)
            out_ref[at, lanes(chunk)] = (
                inner[:SPAN] + outer[at] * carried[:SPAN] + skip * x_part
            ).astype(BF16)
            from_block = inner[SPAN:] if s == 0 else from_block + inner[SPAN:]
            from_carried = (
                carried[SPAN:]
                if s == 0
                else jnp.where(spot_span == s, carried[SPAN:], from_carried)
            )
        state_part = spread(spot_parts, expand) * from_carried + from_block
        xd_part = x_dec[:, lanes(chunk)]
        value = spread(running_parts, expand) * state_part + skip * xd_part.astype(F32)
        for k in range(STEPS):
            value = value + spread(fresh_parts[k], expand) * dot(fresh_pick[k], xd_part)
        res[:, lanes(chunk)] = jnp.where(present, value, 0.0)
        for part in range(LANES // HOP // 2, LANES // HOP):
            relay(hop + LANES // HOP + part)
        if chunk + 1 in ends:
            piece = ends.index(chunk + 1)
            begin = ends[piece - 1] if piece else 0
            area = slice(begin * LANES, (chunk + 1) * LANES)
            for q in range(seq_count):
                dres[piece, q, :, : area.stop - area.start] = res[
                    pl.ds(q * STEPS, STEPS), area
                ].astype(BF16)
            leaving.append((area, exchange(
                dres.at[piece], rres.at[piece], send_out.at[piece], recv_out.at[piece]
            )))

    for piece, (area, copies) in enumerate(leaving):
        for copy in copies:
            copy.wait()
        rres[piece, me] = dres[piece, me]
        dout_ref[0, :, :, area] = rres[piece, :, :, : area.stop - area.start]
    if seq_count > 1:

        @pl.when(me < seq_count - 1)
        def _():
            for hop in range(hops):
                onward(hop).wait_send()


def shards(
    ssm_input, bmat, cmat, dt_raw, a_log, d_skip, prompt_len, owner, dec_x, dec_b, dec_c, dec_dt
):
    seq_count = lax.axis_size("seq")
    tokens, width = ssm_input.shape
    heads = dt_raw.shape[1]
    gn = bmat.shape[1]
    spans = tokens // SPAN
    hops = width // HOP
    half = width // 2
    rows = seq_count * STEPS
    vmem = pl.BlockSpec(memory_space=pltpu.VMEM)
    dma = pltpu.SemaphoreType.DMA
    slots = (seq_count, STEPS)
    return pl.pallas_call(
        functools.partial(kernel, seq_count),
        out_shape=(
            jax.ShapeDtypeStruct((tokens, width), BF16),
            jax.ShapeDtypeStruct((1,) + slots + (width,), BF16),
        ),
        in_specs=[pl.BlockSpec(memory_space=pltpu.HBM)] * 3 + [vmem] * 9,
        out_specs=(vmem, vmem),
        scratch_shapes=[
            pltpu.VMEM((tokens, width), BF16),
            pltpu.VMEM((tokens, gn), BF16),
            pltpu.VMEM((tokens, gn), BF16),
            pltpu.VMEM(slots + (width,), BF16),
            pltpu.VMEM(slots + (gn,), BF16),
            pltpu.VMEM(slots + (gn,), BF16),
            pltpu.VMEM(slots + (heads,), BF16),
            pltpu.VMEM((rows, width), F32),
            pltpu.VMEM((rows, gn), F32),
            pltpu.VMEM((rows, gn), F32),
            pltpu.VMEM((rows, heads), F32),
            pltpu.VMEM((rows, width), F32),
            pltpu.VMEM((3,) + slots + (half,), BF16),
            pltpu.VMEM((3,) + slots + (half,), BF16),
            pltpu.VMEM((hops, N, HOP), BF16),
            pltpu.VMEM((hops, N, HOP), BF16),
            pltpu.VMEM((max(spans - 1, 1), N, width), F32),
            pltpu.VMEM((N, width), F32),
            dma((3,)),
            dma((4, seq_count)),
            dma((4, seq_count)),
            dma((4,)),
            dma((hops,)),
            dma((hops,)),
            dma((3, seq_count)),
            dma((3, seq_count)),
        ],
        compiler_params=pltpu.CompilerParams(
            collective_id=0, has_side_effects=True, vmem_limit_bytes=40 * 1024 * 1024
        ),
    )(
        ssm_input, bmat, cmat, dt_raw.T, a_log[None, :], d_skip[None, :],
        prompt_len[None, :], owner[None, :], dec_x, dec_b, dec_c, dec_dt,
    )


def solution(mesh):
    placed = (
        P(("grp", "seq"), "tp"),
        P(("grp", "seq"), "tp"),
        P(("grp", "seq"), "tp"),
        P(("grp", "seq"), "tp"),
        P("tp"),
        P("tp"),
        P("grp"),
        P("grp"),
        P(("grp", "seq"), None, None, "tp"),
        P(("grp", "seq"), None, None, "tp"),
        P(("grp", "seq"), None, None, "tp"),
        P(("grp", "seq"), None, None, "tp"),
    )
    return jax.shard_map(
        shards,
        mesh=mesh,
        in_specs=placed,
        out_specs=(P(("grp", "seq"), "tp"), P(("grp", "seq"), None, None, "tp")),
        check_vma=False,
    )
```

```python
import functools

import jax
import jax.numpy as jnp
from jax import lax
from jax.experimental import pallas as pl
from jax.experimental.pallas import tpu as pltpu
from jax.sharding import PartitionSpec as P

H = 128
P_SIZE = 64
N = 128
G = 8
SPAN = 128
STEPS = 4
LANES = 256
HOP = 128
MESH = pl.DeviceIdType.MESH
F32 = jnp.float32
BF16 = jnp.bfloat16
FAR = -1e30


def iota(shape, axis):
    return lax.broadcasted_iota(jnp.int32, shape, axis)


def dot(a, b):
    return jnp.dot(a, b, preferred_element_type=F32)


def dot_t(a, b):
    return lax.dot_general(a, b, (((1,), (1,)), ((), ())), preferred_element_type=F32)


def halves(value, count):
    pieces = []
    for _ in range(count):
        piece = value.astype(BF16)
        pieces.append(piece)
        value = value - piece.astype(F32)
    return pieces


def picked(selector, value, count=3):
    parts = [dot(selector, piece) for piece in halves(value, count)]
    return sum(parts[1:], parts[0])


def spread(pieces, expand):
    parts = [dot(piece, expand) for piece in pieces]
    return sum(parts[1:], parts[0])


def ones(mask):
    return jnp.where(mask, 1.0, 0.0).astype(BF16)


def softplus(value):
    return jnp.maximum(value, 0.0) + jnp.log1p(jnp.exp(-jnp.abs(value)))


def kernel(
    seq_count,
    x_hbm, b_hbm, c_hbm, dt_ref, alog_ref, skip_ref, len_ref, own_ref,
    dx_ref, db_ref, dc_ref, ddt_ref,
    out_hbm, dout_ref,
    x_ref, b_ref, c_ref, out_ref, rx, rb, rc, rdt, xd, bd, cd, dtd, res, dres, rres,
    inbuf, outbuf, first, total,
    load_sem, store_sem, send_in, recv_in, own_sem, send_state, recv_state, send_out, recv_out,
):
    me = lax.axis_index("seq")
    tokens, width = x_ref.shape
    heads = dt_ref.shape[0]
    groups = b_ref.shape[1] // N
    per_group = heads // groups
    spans = tokens // SPAN
    chunks = width // LANES
    heads_chunk = LANES // P_SIZE
    rows = seq_count * STEPS

    barrier = pltpu.get_barrier_semaphore()
    for d in range(1, seq_count):
        pl.semaphore_signal(
            barrier, inc=1, device_id={"seq": lax.rem(me + d, seq_count)}, device_id_type=MESH
        )
    loads = [
        pltpu.make_async_copy(source, landing, load_sem.at[k])
        for k, (source, landing) in enumerate(((x_hbm, x_ref), (b_hbm, b_ref), (c_hbm, c_ref)))
    ]
    for copy in loads:
        copy.start()

    step_t = softplus(dt_ref[...].astype(F32))
    step = step_t.T
    rate = -jnp.exp(alog_ref[...])
    t_row, t_col = iota((tokens, tokens), 0), iota((tokens, tokens), 1)
    same = (t_row // SPAN) == (t_col // SPAN)
    cum = picked(ones(same & (t_col <= t_row)), rate * step)
    last = [cum[(s + 1) * SPAN - 1:(s + 1) * SPAN, :] for s in range(spans)]
    into = jnp.concatenate(
        [
            jnp.exp(last[s] - cum[s * SPAN:(s + 1) * SPAN]) * step[s * SPAN:(s + 1) * SPAN]
            for s in range(spans)
        ],
        axis=0,
    )
    into_parts = halves(into, 2)
    grown = [halves(jnp.exp(last[s]), 2) for s in range(spans)]
    outer_parts = halves(jnp.exp(cum), 2)
    cum_t = cum.T

    def exchange(source, landing, sends, recvs):
        copies = []
        for d in range(1, seq_count):
            target = lax.rem(me + d, seq_count)
            copies.append(
                pltpu.make_async_remote_copy(
                    src_ref=source.at[target],
                    dst_ref=landing.at[me],
                    send_sem=sends.at[d],
                    recv_sem=recvs.at[d],
                    device_id={"seq": target},
                    device_id_type=MESH,
                )
            )
        for copy in copies:
            copy.start()
        return copies

    def expander(chunk):
        return ones(iota((heads, LANES), 0) == iota((heads, LANES), 1) // P_SIZE + chunk * heads_chunk)

    def lanes(chunk):
        return slice(chunk * LANES, (chunk + 1) * LANES)

    pl.semaphore_wait(barrier, seq_count - 1)
    arriving = []
    for k, (source, landing) in enumerate(
        ((dx_ref, rx), (db_ref, rb), (dc_ref, rc), (ddt_ref, rdt))
    ):
        arriving += exchange(source.at[0], landing, send_in.at[k], recv_in.at[k])
        mine_copy = pltpu.make_async_copy(source.at[0, me], landing.at[me], own_sem.at[k])
        mine_copy.start()
        arriving.append(mine_copy)
    for copy in loads:
        copy.wait()
    b_t = [
        [b_ref[s * SPAN:(s + 1) * SPAN, g * N:(g + 1) * N].T for g in range(groups)]
        for s in range(spans)
    ]
    hops = width // HOP

    def hop_lanes(hop):
        return slice(hop * HOP, (hop + 1) * HOP)

    def onward(hop):
        return pltpu.make_async_remote_copy(
            src_ref=outbuf.at[hop],
            dst_ref=inbuf.at[hop],
            send_sem=send_state.at[hop],
            recv_sem=recv_state.at[hop],
            device_id={"seq": lax.rem(me + 1, seq_count)},
            device_id_type=MESH,
        )

    for chunk in range(chunks):
        g = chunk * heads_chunk // per_group
        expand = expander(chunk)
        weighted = (x_ref[:, lanes(chunk)].astype(F32) * spread(into_parts, expand)).astype(BF16)
        state = None
        for s in range(spans):
            own = dot(b_t[s][g], weighted[s * SPAN:(s + 1) * SPAN])
            state = own if state is None else spread(grown[s], expand) * state + own
            if s < spans - 1:
                first[s, :, lanes(chunk)] = state
        total[:, lanes(chunk)] = state

        @pl.when(me == 0)
        def _():
            for part in range(LANES // HOP):
                hop = chunk * (LANES // HOP) + part
                outbuf[hop] = state[:, hop_lanes(part)].astype(BF16)
                inbuf[hop] = jnp.zeros(inbuf.shape[1:], BF16)
                if seq_count > 1:
                    onward(hop).start()

    def relay(hop):
        if seq_count == 1 or hop >= hops:
            return
        chunk, part = hop * HOP // LANES, hop % (LANES // HOP)

        @pl.when((me > 0) & (me < seq_count - 1))
        def _():
            onward(hop).wait_recv()
            expand = expander(chunk)[:, hop_lanes(part)]
            through = spread(grown[0], expand)
            for s in range(1, spans):
                through = through * spread(grown[s], expand)
            outbuf[hop] = (
                through * inbuf[hop].astype(F32) + total[:, hop_lanes(hop)]
            ).astype(BF16)
            onward(hop).start()

    for hop in range(LANES // HOP):
        relay(hop)

    for copy in arriving:
        copy.wait()
    for q in range(seq_count):
        part = pl.ds(q * STEPS, STEPS)
        xd[part, :] = rx[q].astype(F32)
        bd[part, :] = rb[q].astype(F32)
        cd[part, :] = rc[q].astype(F32)
        dtd[part, :] = rdt[q].astype(F32)
    requests = len_ref.shape[1]
    final = len_ref[...] - 1
    here = (final >= me * tokens) & (final < (me + 1) * tokens)
    chosen = here & (own_ref[...] == iota((rows, requests), 0) // STEPS)
    spot = jnp.sum(jnp.where(chosen, final - me * tokens, 0), axis=1, keepdims=True)
    present = jnp.sum(jnp.where(chosen, 1, 0), axis=1, keepdims=True) > 0
    place = iota((rows, tokens), 1)
    upto = (place <= spot) & (place // SPAN == spot // SPAN)
    cum_spot = picked(ones(place == spot), cum)
    spot_span = spot // SPAN
    spot_parts = halves(jnp.exp(cum_spot), 2)
    dstep = softplus(dtd[...])
    r_row, r_col = iota((rows, rows), 0), iota((rows, rows), 1)
    slot = (r_row // STEPS) == (r_col // STEPS)
    running = picked(ones(slot & (r_col <= r_row)), rate * dstep)
    running_parts = halves(jnp.exp(running), 2)
    c_dec = cd[...].astype(BF16)
    b_dec = bd[...].astype(BF16)
    x_dec = xd[...].astype(BF16)
    head_group = iota((rows, heads), 1) // per_group
    pairs = [
        dot_t(c_dec[:, g * N:(g + 1) * N], b_dec[:, g * N:(g + 1) * N]) for g in range(groups)
    ]
    step_row = iota((rows, heads), 0) % STEPS
    fresh_parts, fresh_pick = [], []
    for k in range(STEPS):
        chosen_k = slot & (r_col % STEPS == k)
        pick = ones(chosen_k)
        score = jnp.zeros((rows, heads), F32)
        for g in range(groups):
            value = jnp.sum(jnp.where(chosen_k, pairs[g], 0.0), axis=1, keepdims=True)
            score = jnp.where(head_group == g, value, score)
        gap = jnp.where(step_row >= k, running - picked(pick, running), FAR)
        fresh_parts.append(halves(jnp.exp(gap) * picked(pick, dstep) * score, 2))
        fresh_pick.append(pick)
    skip_parts = halves(skip_ref[...], 3)

    scores, dec_scores = [], []
    for s in range(spans):
        at = slice(s * SPAN, (s + 1) * SPAN)
        scores.append([])
        dec_scores.append([])
        for g in range(groups):
            cols = slice(g * N, (g + 1) * N)
            scores[s].append(dot_t(c_ref[at, cols], b_ref[at, cols]))
            dec_scores[s].append(dot_t(c_dec[:, cols], b_ref[at, cols]))
    causal = iota((SPAN, SPAN), 0) >= iota((SPAN, SPAN), 1)
    low = ones(iota((1, 2 * P_SIZE), 1) < P_SIZE)
    high = ones(iota((1, 2 * P_SIZE), 1) >= P_SIZE)

    def weights(head, s):
        g = head // per_group
        at = slice(s * SPAN, (s + 1) * SPAN)
        row = cum_t[head:head + 1, at]
        size = step_t[head:head + 1, at]
        gap = jnp.where(causal, cum[at, head:head + 1] - row, FAR)
        main = scores[s][g] * jnp.exp(gap) * size
        gap = jnp.where(upto[:, at], cum_spot[:, head:head + 1] - row, FAR)
        extra = dec_scores[s][g] * jnp.exp(gap) * size
        return jnp.concatenate([main.astype(BF16), extra.astype(BF16)], axis=0)

    ends = [chunks // 2, chunks - 1, chunks]
    leaving, stores = [], []
    for chunk in range(chunks):
        g = chunk * heads_chunk // per_group
        cols = slice(g * N, (g + 1) * N)
        expand = expander(chunk)
        grow = [spread(grown[s], expand) for s in range(spans)]
        inners = []
        for s in range(spans):
            at = slice(s * SPAN, (s + 1) * SPAN)
            inner = []
            for pair in range(heads_chunk // 2):
                head = chunk * heads_chunk + 2 * pair
                start = chunk * LANES + pair * 2 * P_SIZE
                x_pair = x_ref[at, start:start + 2 * P_SIZE]
                both = jnp.concatenate([x_pair * low, x_pair * high], axis=0)
                left = jnp.concatenate([weights(head, s), weights(head + 1, s)], axis=1)
                inner.append(dot(left, both))
            inners.append(jnp.concatenate(inner, axis=1))
        hop = chunk * (LANES // HOP)
        for part in range(LANES // HOP // 2):
            relay(hop + LANES // HOP + part)
        if seq_count > 1:

            @pl.when(me == seq_count - 1)
            def _():
                for part in range(LANES // HOP):
                    onward(hop + part).wait_recv()

        incoming = jnp.concatenate([inbuf[hop + part] for part in range(LANES // HOP)], axis=1)
        outer = spread(outer_parts, expand)
        skip = spread(skip_parts, expand)
        from_block = None
        from_carried = None
        reach = incoming.astype(F32)
        passed = None
        for s in range(spans):
            at = slice(s * SPAN, (s + 1) * SPAN)
            inner = inners[s]
            if s == 0:
                held = incoming
            else:
                passed = grow[s - 1] if passed is None else passed * grow[s - 1]
                held = (passed * reach + first[s - 1, :, lanes(chunk)]).astype(BF16)
            carried = dot(jnp.concatenate([c_ref[at, cols], c_dec[:, cols]], axis=0), held)
            x_part = x_ref[at, lanes(chunk)].astype(F32)
            out_ref[at, lanes(chunk)] = (
                inner[:SPAN] + outer[at] * carried[:SPAN] + skip * x_part
            ).astype(BF16)
            from_block = inner[SPAN:] if s == 0 else from_block + inner[SPAN:]
            from_carried = (
                carried[SPAN:]
                if s == 0
                else jnp.where(spot_span == s, carried[SPAN:], from_carried)
            )
        store = pltpu.make_async_copy(
            out_ref.at[:, lanes(chunk)], out_hbm.at[:, lanes(chunk)], store_sem.at[chunk]
        )
        store.start()
        stores.append(store)
        state_part = spread(spot_parts, expand) * from_carried + from_block
        xd_part = x_dec[:, lanes(chunk)]
        value = spread(running_parts, expand) * state_part + skip * xd_part.astype(F32)
        for k in range(STEPS):
            value = value + spread(fresh_parts[k], expand) * dot(fresh_pick[k], xd_part)
        res[:, lanes(chunk)] = jnp.where(present, value, 0.0)
        for part in range(LANES // HOP // 2, LANES // HOP):
            relay(hop + LANES // HOP + part)
        if chunk + 1 in ends:
            piece = ends.index(chunk + 1)
            begin = ends[piece - 1] if piece else 0
            area = slice(begin * LANES, (chunk + 1) * LANES)
            for q in range(seq_count):
                dres[piece, q, :, : area.stop - area.start] = res[
                    pl.ds(q * STEPS, STEPS), area
                ].astype(BF16)
            leaving.append((area, exchange(
                dres.at[piece], rres.at[piece], send_out.at[piece], recv_out.at[piece]
            )))

    for piece, (area, copies) in enumerate(leaving):
        for copy in copies:
            copy.wait()
        rres[piece, me] = dres[piece, me]
        dout_ref[0, :, :, area] = rres[piece, :, :, : area.stop - area.start]
    if seq_count > 1:

        @pl.when(me < seq_count - 1)
        def _():
            for hop in range(hops):
                onward(hop).wait_send()

    for store in stores:
        store.wait()


def shards(
    ssm_input, bmat, cmat, dt_raw, a_log, d_skip, prompt_len, owner, dec_x, dec_b, dec_c, dec_dt
):
    seq_count = lax.axis_size("seq")
    tokens, width = ssm_input.shape
    heads = dt_raw.shape[1]
    gn = bmat.shape[1]
    spans = tokens // SPAN
    hops = width // HOP
    half = width // 2
    rows = seq_count * STEPS
    vmem = pl.BlockSpec(memory_space=pltpu.VMEM)
    dma = pltpu.SemaphoreType.DMA
    slots = (seq_count, STEPS)
    return pl.pallas_call(
        functools.partial(kernel, seq_count),
        out_shape=(
            jax.ShapeDtypeStruct((tokens, width), BF16),
            jax.ShapeDtypeStruct((1,) + slots + (width,), BF16),
        ),
        in_specs=[pl.BlockSpec(memory_space=pltpu.HBM)] * 3 + [vmem] * 9,
        out_specs=(pl.BlockSpec(memory_space=pltpu.HBM), vmem),
        scratch_shapes=[
            pltpu.VMEM((tokens, width), BF16),
            pltpu.VMEM((tokens, gn), BF16),
            pltpu.VMEM((tokens, gn), BF16),
            pltpu.VMEM((tokens, width), BF16),
            pltpu.VMEM(slots + (width,), BF16),
            pltpu.VMEM(slots + (gn,), BF16),
            pltpu.VMEM(slots + (gn,), BF16),
            pltpu.VMEM(slots + (heads,), BF16),
            pltpu.VMEM((rows, width), F32),
            pltpu.VMEM((rows, gn), F32),
            pltpu.VMEM((rows, gn), F32),
            pltpu.VMEM((rows, heads), F32),
            pltpu.VMEM((rows, width), F32),
            pltpu.VMEM((3,) + slots + (half,), BF16),
            pltpu.VMEM((3,) + slots + (half,), BF16),
            pltpu.VMEM((hops, N, HOP), BF16),
            pltpu.VMEM((hops, N, HOP), BF16),
            pltpu.VMEM((max(spans - 1, 1), N, width), F32),
            pltpu.VMEM((N, width), F32),
            dma((3,)),
            dma((width // LANES,)),
            dma((4, seq_count)),
            dma((4, seq_count)),
            dma((4,)),
            dma((hops,)),
            dma((hops,)),
            dma((3, seq_count)),
            dma((3, seq_count)),
        ],
        compiler_params=pltpu.CompilerParams(
            collective_id=0, has_side_effects=True, vmem_limit_bytes=63 * 1024 * 1024
        ),
    )(
        ssm_input, bmat, cmat, dt_raw.T, a_log[None, :], d_skip[None, :],
        prompt_len[None, :], owner[None, :], dec_x, dec_b, dec_c, dec_dt,
    )


def solution(mesh):
    placed = (
        P(("grp", "seq"), "tp"),
        P(("grp", "seq"), "tp"),
        P(("grp", "seq"), "tp"),
        P(("grp", "seq"), "tp"),
        P("tp"),
        P("tp"),
        P("grp"),
        P("grp"),
        P(("grp", "seq"), None, None, "tp"),
        P(("grp", "seq"), None, None, "tp"),
        P(("grp", "seq"), None, None, "tp"),
        P(("grp", "seq"), None, None, "tp"),
    )
    return jax.shard_map(
        shards,
        mesh=mesh,
        in_specs=placed,
        out_specs=(P(("grp", "seq"), "tp"), P(("grp", "seq"), None, None, "tp")),
        check_vma=False,
    )
```

```python
import functools

import jax
import jax.numpy as jnp
from jax import lax
from jax.experimental import pallas as pl
from jax.experimental.pallas import tpu as pltpu
from jax.sharding import PartitionSpec as P

H = 128
P_SIZE = 64
N = 128
G = 8
SPAN = 128
STEPS = 4
LANES = 256
HOP = 128
MESH = pl.DeviceIdType.MESH
F32 = jnp.float32
BF16 = jnp.bfloat16
FAR = -1e30


def iota(shape, axis):
    return lax.broadcasted_iota(jnp.int32, shape, axis)


def dot(a, b):
    return jnp.dot(a, b, preferred_element_type=F32)


def dot_t(a, b):
    return lax.dot_general(a, b, (((1,), (1,)), ((), ())), preferred_element_type=F32)


def halves(value, count):
    pieces = []
    for _ in range(count):
        piece = value.astype(BF16)
        pieces.append(piece)
        value = value - piece.astype(F32)
    return pieces


def picked(selector, value, count=3):
    parts = [dot(selector, piece) for piece in halves(value, count)]
    return sum(parts[1:], parts[0])


def spread(pieces, expand):
    parts = [dot(piece, expand) for piece in pieces]
    return sum(parts[1:], parts[0])


def ones(mask):
    return jnp.where(mask, 1.0, 0.0).astype(BF16)


def softplus(value):
    return jnp.maximum(value, 0.0) + jnp.log1p(jnp.exp(-jnp.abs(value)))


def kernel(
    seq_count,
    x_hbm, b_hbm, c_hbm, dt_ref, alog_ref, skip_ref, len_ref, own_ref,
    dx_ref, db_ref, dc_ref, ddt_ref,
    out_hbm, dout_ref,
    x_ref, b_ref, c_ref, out_ref, rx, rb, rc, rdt, xd, bd, cd, dtd, res, dres, rres,
    inbuf, outbuf, first, total,
    load_sem, store_sem, send_in, recv_in, own_sem, send_state, recv_state, send_out, recv_out,
):
    me = lax.axis_index("seq")
    tokens, width = x_ref.shape
    heads = dt_ref.shape[0]
    groups = b_ref.shape[1] // N
    per_group = heads // groups
    spans = tokens // SPAN
    chunks = width // LANES
    heads_chunk = LANES // P_SIZE
    rows = seq_count * STEPS

    barrier = pltpu.get_barrier_semaphore()
    for d in range(1, seq_count):
        pl.semaphore_signal(
            barrier, inc=1, device_id={"seq": lax.rem(me + d, seq_count)}, device_id_type=MESH
        )
    loads = [
        pltpu.make_async_copy(source, landing, load_sem.at[k])
        for k, (source, landing) in enumerate(((x_hbm, x_ref), (b_hbm, b_ref), (c_hbm, c_ref)))
    ]
    for copy in loads:
        copy.start()

    step_t = softplus(dt_ref[...].astype(F32))
    step = step_t.T
    rate = -jnp.exp(alog_ref[...])
    t_row, t_col = iota((tokens, tokens), 0), iota((tokens, tokens), 1)
    same = (t_row // SPAN) == (t_col // SPAN)
    cum = picked(ones(same & (t_col <= t_row)), rate * step)
    last = [cum[(s + 1) * SPAN - 1:(s + 1) * SPAN, :] for s in range(spans)]
    into = jnp.concatenate(
        [
            jnp.exp(last[s] - cum[s * SPAN:(s + 1) * SPAN]) * step[s * SPAN:(s + 1) * SPAN]
            for s in range(spans)
        ],
        axis=0,
    )
    into_parts = halves(into, 2)
    grown = [halves(jnp.exp(last[s]), 2) for s in range(spans)]
    outer_parts = halves(jnp.exp(cum), 2)
    cum_t = cum.T

    def exchange(source, landing, sends, recvs):
        copies = []
        for d in range(1, seq_count):
            target = lax.rem(me + d, seq_count)
            copies.append(
                pltpu.make_async_remote_copy(
                    src_ref=source.at[target],
                    dst_ref=landing.at[me],
                    send_sem=sends.at[d],
                    recv_sem=recvs.at[d],
                    device_id={"seq": target},
                    device_id_type=MESH,
                )
            )
        for copy in copies:
            copy.start()
        return copies

    def expander(chunk):
        return ones(iota((heads, LANES), 0) == iota((heads, LANES), 1) // P_SIZE + chunk * heads_chunk)

    def lanes(chunk):
        return slice(chunk * LANES, (chunk + 1) * LANES)

    pl.semaphore_wait(barrier, seq_count - 1)
    arriving = []
    for k, (source, landing) in enumerate(
        ((dx_ref, rx), (db_ref, rb), (dc_ref, rc), (ddt_ref, rdt))
    ):
        arriving += exchange(source.at[0], landing, send_in.at[k], recv_in.at[k])
        mine_copy = pltpu.make_async_copy(source.at[0, me], landing.at[me], own_sem.at[k])
        mine_copy.start()
        arriving.append(mine_copy)
    for copy in loads:
        copy.wait()
    b_t = [
        [b_ref[s * SPAN:(s + 1) * SPAN, g * N:(g + 1) * N].T for g in range(groups)]
        for s in range(spans)
    ]
    hops = width // HOP

    def hop_lanes(hop):
        return slice(hop * HOP, (hop + 1) * HOP)

    def onward(hop):
        return pltpu.make_async_remote_copy(
            src_ref=outbuf.at[hop],
            dst_ref=inbuf.at[hop],
            send_sem=send_state.at[hop],
            recv_sem=recv_state.at[hop],
            device_id={"seq": lax.rem(me + 1, seq_count)},
            device_id_type=MESH,
        )

    for chunk in range(chunks):
        g = chunk * heads_chunk // per_group
        expand = expander(chunk)
        weighted = (x_ref[:, lanes(chunk)].astype(F32) * spread(into_parts, expand)).astype(BF16)
        state = None
        for s in range(spans):
            own = dot(b_t[s][g], weighted[s * SPAN:(s + 1) * SPAN])
            state = own if state is None else spread(grown[s], expand) * state + own
            if s < spans - 1:
                first[s, :, lanes(chunk)] = state
        total[:, lanes(chunk)] = state

        @pl.when(me == 0)
        def _():
            for part in range(LANES // HOP):
                hop = chunk * (LANES // HOP) + part
                outbuf[hop] = state[:, hop_lanes(part)].astype(BF16)
                inbuf[hop] = jnp.zeros(inbuf.shape[1:], BF16)
                if seq_count > 1:
                    onward(hop).start()

    def relay(hop):
        if seq_count == 1 or hop >= hops:
            return
        chunk, part = hop * HOP // LANES, hop % (LANES // HOP)

        @pl.when((me > 0) & (me < seq_count - 1))
        def _():
            onward(hop).wait_recv()
            expand = expander(chunk)[:, hop_lanes(part)]
            through = spread(grown[0], expand)
            for s in range(1, spans):
                through = through * spread(grown[s], expand)
            outbuf[hop] = (
                through * inbuf[hop].astype(F32) + total[:, hop_lanes(hop)]
            ).astype(BF16)
            onward(hop).start()

    for hop in range(LANES // HOP):
        relay(hop)

    for copy in arriving:
        copy.wait()
    for q in range(seq_count):
        part = pl.ds(q * STEPS, STEPS)
        xd[part, :] = rx[q].astype(F32)
        bd[part, :] = rb[q].astype(F32)
        cd[part, :] = rc[q].astype(F32)
        dtd[part, :] = rdt[q].astype(F32)
    requests = len_ref.shape[1]
    final = len_ref[...] - 1
    here = (final >= me * tokens) & (final < (me + 1) * tokens)
    chosen = here & (own_ref[...] == iota((rows, requests), 0) // STEPS)
    spot = jnp.sum(jnp.where(chosen, final - me * tokens, 0), axis=1, keepdims=True)
    present = jnp.sum(jnp.where(chosen, 1, 0), axis=1, keepdims=True) > 0
    place = iota((rows, tokens), 1)
    upto = (place <= spot) & (place // SPAN == spot // SPAN)
    cum_spot = picked(ones(place == spot), cum)
    spot_span = spot // SPAN
    spot_parts = halves(jnp.exp(cum_spot), 2)
    dstep = softplus(dtd[...])
    r_row, r_col = iota((rows, rows), 0), iota((rows, rows), 1)
    slot = (r_row // STEPS) == (r_col // STEPS)
    running = picked(ones(slot & (r_col <= r_row)), rate * dstep)
    running_parts = halves(jnp.exp(running), 2)
    c_dec = cd[...].astype(BF16)
    b_dec = bd[...].astype(BF16)
    x_dec = xd[...].astype(BF16)
    head_group = iota((rows, heads), 1) // per_group
    pairs = [
        dot_t(c_dec[:, g * N:(g + 1) * N], b_dec[:, g * N:(g + 1) * N]) for g in range(groups)
    ]
    step_row = iota((rows, heads), 0) % STEPS
    fresh_parts, fresh_pick = [], []
    for k in range(STEPS):
        chosen_k = slot & (r_col % STEPS == k)
        pick = ones(chosen_k)
        score = jnp.zeros((rows, heads), F32)
        for g in range(groups):
            value = jnp.sum(jnp.where(chosen_k, pairs[g], 0.0), axis=1, keepdims=True)
            score = jnp.where(head_group == g, value, score)
        gap = jnp.where(step_row >= k, running - picked(pick, running), FAR)
        fresh_parts.append(halves(jnp.exp(gap) * picked(pick, dstep) * score, 2))
        fresh_pick.append(pick)
    skip_parts = halves(skip_ref[...], 3)

    scores, dec_scores = [], []
    for s in range(spans):
        at = slice(s * SPAN, (s + 1) * SPAN)
        scores.append([])
        dec_scores.append([])
        for g in range(groups):
            cols = slice(g * N, (g + 1) * N)
            scores[s].append(dot_t(c_ref[at, cols], b_ref[at, cols]))
            dec_scores[s].append(dot_t(c_dec[:, cols], b_ref[at, cols]))
    causal = iota((SPAN, SPAN), 0) >= iota((SPAN, SPAN), 1)
    low = ones(iota((1, 2 * P_SIZE), 1) < P_SIZE)
    high = ones(iota((1, 2 * P_SIZE), 1) >= P_SIZE)

    def weights(head, s):
        g = head // per_group
        at = slice(s * SPAN, (s + 1) * SPAN)
        row = cum_t[head:head + 1, at]
        size = step_t[head:head + 1, at]
        gap = jnp.where(causal, cum[at, head:head + 1] - row, FAR)
        main = scores[s][g] * jnp.exp(gap) * size
        gap = jnp.where(upto[:, at], cum_spot[:, head:head + 1] - row, FAR)
        extra = dec_scores[s][g] * jnp.exp(gap) * size
        return jnp.concatenate([main.astype(BF16), extra.astype(BF16)], axis=0)

    ends = [chunks]
    leaving, stores = [], []
    for chunk in range(chunks):
        g = chunk * heads_chunk // per_group
        cols = slice(g * N, (g + 1) * N)
        expand = expander(chunk)
        grow = [spread(grown[s], expand) for s in range(spans)]
        inners = []
        for s in range(spans):
            at = slice(s * SPAN, (s + 1) * SPAN)
            inner = []
            for pair in range(heads_chunk // 2):
                head = chunk * heads_chunk + 2 * pair
                start = chunk * LANES + pair * 2 * P_SIZE
                x_pair = x_ref[at, start:start + 2 * P_SIZE]
                both = jnp.concatenate([x_pair * low, x_pair * high], axis=0)
                left = jnp.concatenate([weights(head, s), weights(head + 1, s)], axis=1)
                inner.append(dot(left, both))
            inners.append(jnp.concatenate(inner, axis=1))
        hop = chunk * (LANES // HOP)
        for part in range(LANES // HOP // 2):
            relay(hop + LANES // HOP + part)
        if seq_count > 1:

            @pl.when(me == seq_count - 1)
            def _():
                for part in range(LANES // HOP):
                    onward(hop + part).wait_recv()

        incoming = jnp.concatenate([inbuf[hop + part] for part in range(LANES // HOP)], axis=1)
        outer = spread(outer_parts, expand)
        skip = spread(skip_parts, expand)
        from_block = None
        from_carried = None
        reach = incoming.astype(F32)
        passed = None
        for s in range(spans):
            at = slice(s * SPAN, (s + 1) * SPAN)
            inner = inners[s]
            if s == 0:
                held = incoming
            else:
                passed = grow[s - 1] if passed is None else passed * grow[s - 1]
                held = (passed * reach + first[s - 1, :, lanes(chunk)]).astype(BF16)
            carried = dot(jnp.concatenate([c_ref[at, cols], c_dec[:, cols]], axis=0), held)
            x_part = x_ref[at, lanes(chunk)].astype(F32)
            out_ref[at, lanes(chunk)] = (
                inner[:SPAN] + outer[at] * carried[:SPAN] + skip * x_part
            ).astype(BF16)
            from_block = inner[SPAN:] if s == 0 else from_block + inner[SPAN:]
            from_carried = (
                carried[SPAN:]
                if s == 0
                else jnp.where(spot_span == s, carried[SPAN:], from_carried)
            )
        store = pltpu.make_async_copy(
            out_ref.at[:, lanes(chunk)], out_hbm.at[:, lanes(chunk)], store_sem.at[chunk]
        )
        store.start()
        stores.append(store)
        state_part = spread(spot_parts, expand) * from_carried + from_block
        xd_part = x_dec[:, lanes(chunk)]
        value = spread(running_parts, expand) * state_part + skip * xd_part.astype(F32)
        for k in range(STEPS):
            value = value + spread(fresh_parts[k], expand) * dot(fresh_pick[k], xd_part)
        res[:, lanes(chunk)] = jnp.where(present, value, 0.0)
        for part in range(LANES // HOP // 2, LANES // HOP):
            relay(hop + LANES // HOP + part)
        if chunk + 1 in ends:
            piece = ends.index(chunk + 1)
            begin = ends[piece - 1] if piece else 0
            area = slice(begin * LANES, (chunk + 1) * LANES)
            for q in range(seq_count):
                dres[piece, q, :, : area.stop - area.start] = res[
                    pl.ds(q * STEPS, STEPS), area
                ].astype(BF16)
            leaving.append((area, exchange(
                dres.at[piece], rres.at[piece], send_out.at[piece], recv_out.at[piece]
            )))

    for piece, (area, copies) in enumerate(leaving):
        for copy in copies:
            copy.wait()
        rres[piece, me] = dres[piece, me]
        dout_ref[0, :, :, area] = rres[piece, :, :, : area.stop - area.start]
    if seq_count > 1:

        @pl.when(me < seq_count - 1)
        def _():
            for hop in range(hops):
                onward(hop).wait_send()

    for store in stores:
        store.wait()


def shards(
    ssm_input, bmat, cmat, dt_raw, a_log, d_skip, prompt_len, owner, dec_x, dec_b, dec_c, dec_dt
):
    seq_count = lax.axis_size("seq")
    tokens, width = ssm_input.shape
    heads = dt_raw.shape[1]
    gn = bmat.shape[1]
    spans = tokens // SPAN
    hops = width // HOP
    half = width
    rows = seq_count * STEPS
    vmem = pl.BlockSpec(memory_space=pltpu.VMEM)
    dma = pltpu.SemaphoreType.DMA
    slots = (seq_count, STEPS)
    return pl.pallas_call(
        functools.partial(kernel, seq_count),
        out_shape=(
            jax.ShapeDtypeStruct((tokens, width), BF16),
            jax.ShapeDtypeStruct((1,) + slots + (width,), BF16),
        ),
        in_specs=[pl.BlockSpec(memory_space=pltpu.HBM)] * 3 + [vmem] * 9,
        out_specs=(pl.BlockSpec(memory_space=pltpu.HBM), vmem),
        scratch_shapes=[
            pltpu.VMEM((tokens, width), BF16),
            pltpu.VMEM((tokens, gn), BF16),
            pltpu.VMEM((tokens, gn), BF16),
            pltpu.VMEM((tokens, width), BF16),
            pltpu.VMEM(slots + (width,), BF16),
            pltpu.VMEM(slots + (gn,), BF16),
            pltpu.VMEM(slots + (gn,), BF16),
            pltpu.VMEM(slots + (heads,), BF16),
            pltpu.VMEM((rows, width), F32),
            pltpu.VMEM((rows, gn), F32),
            pltpu.VMEM((rows, gn), F32),
            pltpu.VMEM((rows, heads), F32),
            pltpu.VMEM((rows, width), F32),
            pltpu.VMEM((3,) + slots + (half,), BF16),
            pltpu.VMEM((3,) + slots + (half,), BF16),
            pltpu.VMEM((hops, N, HOP), BF16),
            pltpu.VMEM((hops, N, HOP), BF16),
            pltpu.VMEM((max(spans - 1, 1), N, width), F32),
            pltpu.VMEM((N, width), F32),
            dma((3,)),
            dma((width // LANES,)),
            dma((4, seq_count)),
            dma((4, seq_count)),
            dma((4,)),
            dma((hops,)),
            dma((hops,)),
            dma((3, seq_count)),
            dma((3, seq_count)),
        ],
        compiler_params=pltpu.CompilerParams(
            collective_id=0, has_side_effects=True, vmem_limit_bytes=63 * 1024 * 1024
        ),
    )(
        ssm_input, bmat, cmat, dt_raw.T, a_log[None, :], d_skip[None, :],
        prompt_len[None, :], owner[None, :], dec_x, dec_b, dec_c, dec_dt,
    )


def solution(mesh):
    placed = (
        P(("grp", "seq"), "tp"),
        P(("grp", "seq"), "tp"),
        P(("grp", "seq"), "tp"),
        P(("grp", "seq"), "tp"),
        P("tp"),
        P("tp"),
        P("grp"),
        P("grp"),
        P(("grp", "seq"), None, None, "tp"),
        P(("grp", "seq"), None, None, "tp"),
        P(("grp", "seq"), None, None, "tp"),
        P(("grp", "seq"), None, None, "tp"),
    )
    return jax.shard_map(
        shards,
        mesh=mesh,
        in_specs=placed,
        out_specs=(P(("grp", "seq"), "tp"), P(("grp", "seq"), None, None, "tp")),
        check_vma=False,
    )
```

```python
import functools

import jax
import jax.numpy as jnp
from jax import lax
from jax.experimental import pallas as pl
from jax.experimental.pallas import tpu as pltpu
from jax.sharding import PartitionSpec as P

H = 128
P_SIZE = 64
N = 128
G = 8
SPAN = 128
STEPS = 4
LANES = 256
HOP = 128
MESH = pl.DeviceIdType.MESH
F32 = jnp.float32
BF16 = jnp.bfloat16
FAR = -1e30


def iota(shape, axis):
    return lax.broadcasted_iota(jnp.int32, shape, axis)


def dot(a, b):
    return jnp.dot(a, b, preferred_element_type=F32)


def dot_t(a, b):
    return lax.dot_general(a, b, (((1,), (1,)), ((), ())), preferred_element_type=F32)


def halves(value, count):
    pieces = []
    for _ in range(count):
        piece = value.astype(BF16)
        pieces.append(piece)
        value = value - piece.astype(F32)
    return pieces


def picked(selector, value, count=3):
    parts = [dot(selector, piece) for piece in halves(value, count)]
    return sum(parts[1:], parts[0])


def spread(pieces, expand):
    parts = [dot(piece, expand) for piece in pieces]
    return sum(parts[1:], parts[0])


def ones(mask):
    return jnp.where(mask, 1.0, 0.0).astype(BF16)


def softplus(value):
    return jnp.maximum(value, 0.0) + jnp.log1p(jnp.exp(-jnp.abs(value)))


def kernel(
    seq_count,
    x_hbm, b_hbm, c_hbm, dt_ref, alog_ref, skip_ref, len_ref, own_ref,
    dx_ref, db_ref, dc_ref, ddt_ref,
    out_hbm, dout_ref,
    x_ref, b_ref, c_ref, out_ref, rx, rb, rc, rdt, xd, bd, cd, dtd, res, dres, rres,
    inbuf, outbuf, first, total,
    load_sem, store_sem, send_in, recv_in, own_sem, send_state, recv_state, send_out, recv_out,
):
    me = lax.axis_index("seq")
    tokens, width = x_ref.shape
    heads = dt_ref.shape[0]
    groups = b_ref.shape[1] // N
    per_group = heads // groups
    spans = tokens // SPAN
    chunks = width // LANES
    heads_chunk = LANES // P_SIZE
    rows = seq_count * STEPS

    barrier = pltpu.get_barrier_semaphore()
    for d in range(1, seq_count):
        pl.semaphore_signal(
            barrier, inc=1, device_id={"seq": lax.rem(me + d, seq_count)}, device_id_type=MESH
        )
    loads = [
        pltpu.make_async_copy(source, landing, load_sem.at[k])
        for k, (source, landing) in enumerate(((x_hbm, x_ref), (b_hbm, b_ref), (c_hbm, c_ref)))
    ]
    for copy in loads:
        copy.start()

    step_t = softplus(dt_ref[...].astype(F32))
    step = step_t.T
    rate = -jnp.exp(alog_ref[...])
    t_row, t_col = iota((tokens, tokens), 0), iota((tokens, tokens), 1)
    same = (t_row // SPAN) == (t_col // SPAN)
    cum = picked(ones(same & (t_col <= t_row)), rate * step)
    last = [cum[(s + 1) * SPAN - 1:(s + 1) * SPAN, :] for s in range(spans)]
    into = jnp.concatenate(
        [
            jnp.exp(last[s] - cum[s * SPAN:(s + 1) * SPAN]) * step[s * SPAN:(s + 1) * SPAN]
            for s in range(spans)
        ],
        axis=0,
    )
    into_parts = halves(into, 2)
    grown = [halves(jnp.exp(last[s]), 2) for s in range(spans)]
    outer_parts = halves(jnp.exp(cum), 2)
    cum_t = cum.T

    def exchange(source, landing, sends, recvs):
        copies = []
        for d in range(1, seq_count):
            target = lax.rem(me + d, seq_count)
            copies.append(
                pltpu.make_async_remote_copy(
                    src_ref=source.at[target],
                    dst_ref=landing.at[me],
                    send_sem=sends.at[d],
                    recv_sem=recvs.at[d],
                    device_id={"seq": target},
                    device_id_type=MESH,
                )
            )
        for copy in copies:
            copy.start()
        return copies

    def expander(chunk):
        return ones(iota((heads, LANES), 0) == iota((heads, LANES), 1) // P_SIZE + chunk * heads_chunk)

    def lanes(chunk):
        return slice(chunk * LANES, (chunk + 1) * LANES)

    pl.semaphore_wait(barrier, seq_count - 1)
    arriving = []
    for k, (source, landing) in enumerate(
        ((dx_ref, rx), (db_ref, rb), (dc_ref, rc), (ddt_ref, rdt))
    ):
        arriving += exchange(source.at[0], landing, send_in.at[k], recv_in.at[k])
        mine_copy = pltpu.make_async_copy(source.at[0, me], landing.at[me], own_sem.at[k])
        mine_copy.start()
        arriving.append(mine_copy)
    for copy in loads:
        copy.wait()
    b_t = [
        [b_ref[s * SPAN:(s + 1) * SPAN, g * N:(g + 1) * N].T for g in range(groups)]
        for s in range(spans)
    ]
    hops = width // HOP

    def hop_lanes(hop):
        return slice(hop * HOP, (hop + 1) * HOP)

    def onward(hop):
        return pltpu.make_async_remote_copy(
            src_ref=outbuf.at[hop],
            dst_ref=inbuf.at[hop],
            send_sem=send_state.at[hop],
            recv_sem=recv_state.at[hop],
            device_id={"seq": lax.rem(me + 1, seq_count)},
            device_id_type=MESH,
        )

    for chunk in range(chunks):
        g = chunk * heads_chunk // per_group
        expand = expander(chunk)
        weighted = (x_ref[:, lanes(chunk)].astype(F32) * spread(into_parts, expand)).astype(BF16)
        state = None
        for s in range(spans):
            own = dot(b_t[s][g], weighted[s * SPAN:(s + 1) * SPAN])
            state = own if state is None else spread(grown[s], expand) * state + own
            if s < spans - 1:
                first[s, :, lanes(chunk)] = state
        total[:, lanes(chunk)] = state

        @pl.when(me == 0)
        def _():
            for part in range(LANES // HOP):
                hop = chunk * (LANES // HOP) + part
                outbuf[hop] = state[:, hop_lanes(part)].astype(BF16)
                inbuf[hop] = jnp.zeros(inbuf.shape[1:], BF16)
                if seq_count > 1:
                    onward(hop).start()

    def relay(hop):
        if seq_count == 1 or hop >= hops:
            return
        chunk, part = hop * HOP // LANES, hop % (LANES // HOP)

        @pl.when((me > 0) & (me < seq_count - 1))
        def _():
            onward(hop).wait_recv()
            expand = expander(chunk)[:, hop_lanes(part)]
            through = spread(grown[0], expand)
            for s in range(1, spans):
                through = through * spread(grown[s], expand)
            outbuf[hop] = (
                through * inbuf[hop].astype(F32) + total[:, hop_lanes(hop)]
            ).astype(BF16)
            onward(hop).start()

    for hop in range(LANES // HOP):
        relay(hop)

    for copy in arriving:
        copy.wait()
    for q in range(seq_count):
        part = pl.ds(q * STEPS, STEPS)
        xd[part, :] = rx[q].astype(F32)
        bd[part, :] = rb[q].astype(F32)
        cd[part, :] = rc[q].astype(F32)
        dtd[part, :] = rdt[q].astype(F32)
    requests = len_ref.shape[1]
    final = len_ref[...] - 1
    here = (final >= me * tokens) & (final < (me + 1) * tokens)
    chosen = here & (own_ref[...] == iota((rows, requests), 0) // STEPS)
    spot = jnp.sum(jnp.where(chosen, final - me * tokens, 0), axis=1, keepdims=True)
    present = jnp.sum(jnp.where(chosen, 1, 0), axis=1, keepdims=True) > 0
    place = iota((rows, tokens), 1)
    upto = (place <= spot) & (place // SPAN == spot // SPAN)
    cum_spot = picked(ones(place == spot), cum)
    spot_span = spot // SPAN
    spot_parts = halves(jnp.exp(cum_spot), 2)
    dstep = softplus(dtd[...])
    r_row, r_col = iota((rows, rows), 0), iota((rows, rows), 1)
    slot = (r_row // STEPS) == (r_col // STEPS)
    running = picked(ones(slot & (r_col <= r_row)), rate * dstep)
    running_parts = halves(jnp.exp(running), 2)
    c_dec = cd[...].astype(BF16)
    b_dec = bd[...].astype(BF16)
    x_dec = xd[...].astype(BF16)
    head_group = iota((rows, heads), 1) // per_group
    pairs = [
        dot_t(c_dec[:, g * N:(g + 1) * N], b_dec[:, g * N:(g + 1) * N]) for g in range(groups)
    ]
    step_row = iota((rows, heads), 0) % STEPS
    fresh_parts, fresh_pick = [], []
    for k in range(STEPS):
        chosen_k = slot & (r_col % STEPS == k)
        pick = ones(chosen_k)
        score = jnp.zeros((rows, heads), F32)
        for g in range(groups):
            value = jnp.sum(jnp.where(chosen_k, pairs[g], 0.0), axis=1, keepdims=True)
            score = jnp.where(head_group == g, value, score)
        gap = jnp.where(step_row >= k, running - picked(pick, running), FAR)
        fresh_parts.append(halves(jnp.exp(gap) * picked(pick, dstep) * score, 2))
        fresh_pick.append(pick)
    skip_parts = halves(skip_ref[...], 3)

    scores, dec_scores = [], []
    for s in range(spans):
        at = slice(s * SPAN, (s + 1) * SPAN)
        scores.append([])
        dec_scores.append([])
        for g in range(groups):
            cols = slice(g * N, (g + 1) * N)
            scores[s].append(dot_t(c_ref[at, cols], b_ref[at, cols]))
            dec_scores[s].append(dot_t(c_dec[:, cols], b_ref[at, cols]))
    causal = iota((SPAN, SPAN), 0) >= iota((SPAN, SPAN), 1)
    low = ones(iota((1, 2 * P_SIZE), 1) < P_SIZE)
    high = ones(iota((1, 2 * P_SIZE), 1) >= P_SIZE)

    def weights(head, s):
        g = head // per_group
        at = slice(s * SPAN, (s + 1) * SPAN)
        row = cum_t[head:head + 1, at]
        size = step_t[head:head + 1, at]
        gap = jnp.where(causal, cum[at, head:head + 1] - row, FAR)
        main = scores[s][g] * jnp.exp(gap) * size
        gap = jnp.where(upto[:, at], cum_spot[:, head:head + 1] - row, FAR)
        extra = dec_scores[s][g] * jnp.exp(gap) * size
        return jnp.concatenate([main.astype(BF16), extra.astype(BF16)], axis=0)

    ends = [chunks]
    leaving, stores = [], []
    for chunk in range(chunks):
        g = chunk * heads_chunk // per_group
        cols = slice(g * N, (g + 1) * N)
        expand = expander(chunk)
        grow = [spread(grown[s], expand) for s in range(spans)]
        inners = []
        for s in range(spans):
            at = slice(s * SPAN, (s + 1) * SPAN)
            inner = []
            for pair in range(heads_chunk // 2):
                head = chunk * heads_chunk + 2 * pair
                start = chunk * LANES + pair * 2 * P_SIZE
                x_pair = x_ref[at, start:start + 2 * P_SIZE]
                both = jnp.concatenate([x_pair * low, x_pair * high], axis=0)
                left = jnp.concatenate([weights(head, s), weights(head + 1, s)], axis=1)
                inner.append(dot(left, both))
            inners.append(jnp.concatenate(inner, axis=1))
        hop = chunk * (LANES // HOP)
        for part in range(LANES // HOP):
            relay(hop + LANES // HOP + part)
        if seq_count > 1:

            @pl.when(me == seq_count - 1)
            def _():
                for part in range(LANES // HOP):
                    onward(hop + part).wait_recv()

        incoming = jnp.concatenate([inbuf[hop + part] for part in range(LANES // HOP)], axis=1)
        outer = spread(outer_parts, expand)
        skip = spread(skip_parts, expand)
        from_block = None
        from_carried = None
        reach = incoming.astype(F32)
        passed = None
        for s in range(spans):
            at = slice(s * SPAN, (s + 1) * SPAN)
            inner = inners[s]
            if s == 0:
                held = incoming
            else:
                passed = grow[s - 1] if passed is None else passed * grow[s - 1]
                held = (passed * reach + first[s - 1, :, lanes(chunk)]).astype(BF16)
            carried = dot(jnp.concatenate([c_ref[at, cols], c_dec[:, cols]], axis=0), held)
            x_part = x_ref[at, lanes(chunk)].astype(F32)
            out_ref[at, lanes(chunk)] = (
                inner[:SPAN] + outer[at] * carried[:SPAN] + skip * x_part
            ).astype(BF16)
            from_block = inner[SPAN:] if s == 0 else from_block + inner[SPAN:]
            from_carried = (
                carried[SPAN:]
                if s == 0
                else jnp.where(spot_span == s, carried[SPAN:], from_carried)
            )
        store = pltpu.make_async_copy(
            out_ref.at[:, lanes(chunk)], out_hbm.at[:, lanes(chunk)], store_sem.at[chunk]
        )
        store.start()
        stores.append(store)
        state_part = spread(spot_parts, expand) * from_carried + from_block
        xd_part = x_dec[:, lanes(chunk)]
        value = spread(running_parts, expand) * state_part + skip * xd_part.astype(F32)
        for k in range(STEPS):
            value = value + spread(fresh_parts[k], expand) * dot(fresh_pick[k], xd_part)
        res[:, lanes(chunk)] = jnp.where(present, value, 0.0)
        for part in range(0):
            relay(hop + LANES // HOP + part)
        if chunk + 1 in ends:
            piece = ends.index(chunk + 1)
            begin = ends[piece - 1] if piece else 0
            area = slice(begin * LANES, (chunk + 1) * LANES)
            for q in range(seq_count):
                dres[piece, q, :, : area.stop - area.start] = res[
                    pl.ds(q * STEPS, STEPS), area
                ].astype(BF16)
            leaving.append((area, exchange(
                dres.at[piece], rres.at[piece], send_out.at[piece], recv_out.at[piece]
            )))

    for piece, (area, copies) in enumerate(leaving):
        for copy in copies:
            copy.wait()
        rres[piece, me] = dres[piece, me]
        dout_ref[0, :, :, area] = rres[piece, :, :, : area.stop - area.start]
    if seq_count > 1:

        @pl.when(me < seq_count - 1)
        def _():
            for hop in range(hops):
                onward(hop).wait_send()

    for store in stores:
        store.wait()


def shards(
    ssm_input, bmat, cmat, dt_raw, a_log, d_skip, prompt_len, owner, dec_x, dec_b, dec_c, dec_dt
):
    seq_count = lax.axis_size("seq")
    tokens, width = ssm_input.shape
    heads = dt_raw.shape[1]
    gn = bmat.shape[1]
    spans = tokens // SPAN
    hops = width // HOP
    half = width
    rows = seq_count * STEPS
    vmem = pl.BlockSpec(memory_space=pltpu.VMEM)
    dma = pltpu.SemaphoreType.DMA
    slots = (seq_count, STEPS)
    return pl.pallas_call(
        functools.partial(kernel, seq_count),
        out_shape=(
            jax.ShapeDtypeStruct((tokens, width), BF16),
            jax.ShapeDtypeStruct((1,) + slots + (width,), BF16),
        ),
        in_specs=[pl.BlockSpec(memory_space=pltpu.HBM)] * 3 + [vmem] * 9,
        out_specs=(pl.BlockSpec(memory_space=pltpu.HBM), vmem),
        scratch_shapes=[
            pltpu.VMEM((tokens, width), BF16),
            pltpu.VMEM((tokens, gn), BF16),
            pltpu.VMEM((tokens, gn), BF16),
            pltpu.VMEM((tokens, width), BF16),
            pltpu.VMEM(slots + (width,), BF16),
            pltpu.VMEM(slots + (gn,), BF16),
            pltpu.VMEM(slots + (gn,), BF16),
            pltpu.VMEM(slots + (heads,), BF16),
            pltpu.VMEM((rows, width), F32),
            pltpu.VMEM((rows, gn), F32),
            pltpu.VMEM((rows, gn), F32),
            pltpu.VMEM((rows, heads), F32),
            pltpu.VMEM((rows, width), F32),
            pltpu.VMEM((3,) + slots + (half,), BF16),
            pltpu.VMEM((3,) + slots + (half,), BF16),
            pltpu.VMEM((hops, N, HOP), BF16),
            pltpu.VMEM((hops, N, HOP), BF16),
            pltpu.VMEM((max(spans - 1, 1), N, width), F32),
            pltpu.VMEM((N, width), F32),
            dma((3,)),
            dma((width // LANES,)),
            dma((4, seq_count)),
            dma((4, seq_count)),
            dma((4,)),
            dma((hops,)),
            dma((hops,)),
            dma((3, seq_count)),
            dma((3, seq_count)),
        ],
        compiler_params=pltpu.CompilerParams(
            collective_id=0, has_side_effects=True, vmem_limit_bytes=63 * 1024 * 1024
        ),
    )(
        ssm_input, bmat, cmat, dt_raw.T, a_log[None, :], d_skip[None, :],
        prompt_len[None, :], owner[None, :], dec_x, dec_b, dec_c, dec_dt,
    )


def solution(mesh):
    placed = (
        P(("grp", "seq"), "tp"),
        P(("grp", "seq"), "tp"),
        P(("grp", "seq"), "tp"),
        P(("grp", "seq"), "tp"),
        P("tp"),
        P("tp"),
        P("grp"),
        P("grp"),
        P(("grp", "seq"), None, None, "tp"),
        P(("grp", "seq"), None, None, "tp"),
        P(("grp", "seq"), None, None, "tp"),
        P(("grp", "seq"), None, None, "tp"),
    )
    return jax.shard_map(
        shards,
        mesh=mesh,
        in_specs=placed,
        out_specs=(P(("grp", "seq"), "tp"), P(("grp", "seq"), None, None, "tp")),
        check_vma=False,
    )
```
